32 devices in a mesh: outer: 8 (over z, x), inner: 4 (over y, core).
Axes of the slice: x: 2, y: 2, z: 4, core: 2. Of those that a mesh axis runs over, the one named last changes fastest.
Arguments:
- images: bfloat16 [32, 14, 14, 768], P(('outer', 'inner')), may hold values from -6 to 6
- cotangent: bfloat16 [32, 14, 14, 768], P(('outer', 'inner')), may hold values from -20 to 20
- conv_weight: float32 [7, 7, 768], replicated, may hold values from -0.875 to 0.875
- conv_bias: float32 [768], replicated, may hold values from -3 to 3
- norm_gain: float32 [768], replicated, may hold values from 0.1 to 1.9
- norm_bias: float32 [768], replicated, may hold values from -2 to 2
- expand_weight: bfloat16 [768, 3072], replicated, may hold values from -0.21875 to 0.21875
- expand_bias: float32 [3072], replicated, may hold values from -3 to 3
- reduce_weight: bfloat16 [3072, 768], replicated, may hold values from -0.109375 to 0.109375
- layer_scale: float32 [768], replicated, may hold values from 0.2 to 2
- right_first: float32 [3072, 32], replicated, may hold values from -5 to 5
- right_second: float32 [768, 32], replicated, may hold values from -5 to 5
Outputs:
- next_first: float32 [3072, 32], replicated
- next_second: float32 [768, 32], replicated
The draws below stay inside these ranges and needn't reach their ends.
All inputs are finite; a program needn't handle non-finite values.
Results may differ from the reference program's by a relative error of at most 0.009.
Values may be sent and summed in bfloat16 or wider, within the bound.
No kernel may reach another device: no remote copies, remote signals or barrier semaphores. Data moves between devices by JAX's collectives and lax.ppermute only.
A program may use at most 64 MiB of HBM per device.

```python
import math
import jax
import jax.numpy as jnp
from jax import lax

D = 768
FF = 3072
HW = 14
KSIZE = 7
RANK = 32
IMAGES = 32
N_OUTER = 8
N_INNER = 4


def draw_cotangent(key, part):
    scale_key = jax.random.fold_in(key, 11)
    value_key = jax.random.fold_in(key, 12)
    scales = jnp.exp(jax.random.uniform(scale_key, (IMAGES, 1, 1, 1), jnp.float32, jnp.log(0.5), jnp.log(5.0)))
    values = jnp.clip(jax.random.normal(value_key, (IMAGES, HW, HW, D), jnp.float32), -4.0, 4.0)
    return (values * scales).astype(jnp.bfloat16)


def steps_of(own_key, shape, pieces, smallest, top_value):
    def one(position, blocks):
        steps = jax.random.uniform(jax.random.fold_in(jax.random.fold_in(own_key, 6), position), (blocks,), jnp.float32, smallest / len(pieces), top_value / len(pieces))
        return jnp.repeat(jnp.exp(steps), shape[position] // blocks).reshape((-1,) + (1,) * (len(shape) - position - 1))

    level = one(*pieces[0])
    for cut in pieces[1:]:
        level = level * one(*cut)
    return level


def bell_draw(key, shape, scale, limit, cuts=(), dtype=jnp.bfloat16):
    factor_of = steps_of(key, shape, cuts, -0.22, 0.18) if cuts else 1.0
    drawn = jax.random.normal(key, shape, jnp.float32) * scale * factor_of
    return jnp.minimum(jnp.maximum(drawn, -limit), limit).astype(dtype)


def setup_inputs(seed: int = 0) -> dict:
    streams_of = jax.random.split(jax.random.key(seed), 13)
    images = bell_draw(streams_of[0], (IMAGES, HW, HW, D), 1.0, 6.0, ((0, 32),))
    cotangent = draw_cotangent(jax.random.fold_in(streams_of[12], 71), 0)
    conv_weight = bell_draw(streams_of[2], (KSIZE, KSIZE, D), (KSIZE * KSIZE) ** -0.5, 0.875, (), jnp.float32)
    conv_bias = bell_draw(streams_of[3], (D,), 0.5, 3.0, (), jnp.float32)
    norm_gain = jnp.clip(1.0 + 0.18 * jax.random.normal(streams_of[4], (D,), jnp.float32), 0.1, 1.9)
    norm_bias = bell_draw(streams_of[5], (D,), 0.3, 2.0, (), jnp.float32)
    expand_weight = bell_draw(streams_of[6], (D, FF), D ** -0.5, 0.21875)
    expand_bias = bell_draw(streams_of[7], (FF,), 0.5, 3.0, (), jnp.float32)
    reduce_weight = bell_draw(streams_of[8], (FF, D), FF ** -0.5, 0.109375)
    layer_scale = jnp.clip(jnp.exp(jax.random.uniform(streams_of[9], (D,), jnp.float32, math.log(0.2), math.log(2.0))), 0.2, 2.0)
    right_first = bell_draw(streams_of[10], (FF, RANK), 1.0, 5.0, (), jnp.float32)
    right_second = bell_draw(streams_of[11], (D, RANK), 1.0, 5.0, (), jnp.float32)
    return {"images": images, "cotangent": cotangent, "conv_weight": conv_weight, "conv_bias": conv_bias, "norm_gain": norm_gain, "norm_bias": norm_bias, "expand_weight": expand_weight, "expand_bias": expand_bias, "reduce_weight": reduce_weight, "layer_scale": layer_scale, "right_first": right_first, "right_second": right_second}


def depthwise(images, conv_weight, conv_bias):
    kernel = conv_weight.shape[0]
    margin = kernel // 2
    extent = images.shape[1]
    widened = jnp.pad(images.astype(jnp.float32), ((0, 0), (margin, margin), (margin, margin), (0, 0)))
    summed = jnp.zeros(images.shape, jnp.float32) + conv_bias
    for tap_row in range(kernel):
        for tap_col in range(kernel):
            summed = summed + widened[:, tap_row:tap_row + extent, tap_col:tap_col + extent, :] * conv_weight[tap_row, tap_col]
    return summed

def layer_norm(values, norm_gain, norm_bias):
    center = lax.optimization_barrier(jnp.mean(values, axis=-1, keepdims=True))
    spread = lax.optimization_barrier(jnp.mean((values - center) ** 2, axis=-1, keepdims=True))
    return ((values - center) * lax.rsqrt(spread + 1e-06) * norm_gain + norm_bias).astype(jnp.bfloat16)

def gelu_slope(hidden):
    return 0.5 * (1.0 + lax.erf(hidden * 0.7071067811865476)) + hidden * jnp.exp(-0.5 * hidden * hidden) * 0.3989422804014327

def local_rows(images, cotangent, conv_weight, conv_bias, norm_gain, norm_bias, expand_weight, expand_bias, reduce_weight, layer_scale):
    width = images.shape[-1]
    conv_out = depthwise(images, conv_weight, conv_bias).reshape((-1, width))
    normed = layer_norm(conv_out, norm_gain, norm_bias)
    hidden = jnp.dot(normed.astype(jnp.float32), expand_weight.astype(jnp.float32), preferred_element_type=jnp.float32) + expand_bias
    activated = jax.nn.gelu(hidden, approximate=False).astype(jnp.bfloat16)
    out_grad = (cotangent.reshape((-1, width)).astype(jnp.float32) * layer_scale).astype(jnp.bfloat16)
    back = lax.dot_general(out_grad.astype(jnp.float32), reduce_weight.astype(jnp.float32), (((1,), (1,)), ((), ())), preferred_element_type=jnp.float32)
    hid_grad = (back * gelu_slope(hidden)).astype(jnp.bfloat16)
    return (normed, activated, out_grad, hid_grad)

def project(rows_left, rows_right, right):
    thin = jnp.dot(rows_right.astype(jnp.float32), right.astype(jnp.bfloat16).astype(jnp.float32), preferred_element_type=jnp.float32).astype(jnp.bfloat16)
    return lax.dot_general(rows_left.astype(jnp.float32), thin.astype(jnp.float32), (((0,), (0,)), ((), ())), preferred_element_type=jnp.float32)

def back_project(rows_left, rows_right, basis):
    thin = jnp.dot(rows_left.astype(jnp.float32), basis.astype(jnp.bfloat16).astype(jnp.float32), preferred_element_type=jnp.float32).astype(jnp.bfloat16)
    return lax.dot_general(rows_right.astype(jnp.float32), thin.astype(jnp.float32), (((0,), (0,)), ((), ())), preferred_element_type=jnp.float32)

def orthonormal(partial_value):
    gram_matrix = lax.dot_general(partial_value, partial_value, (((0,), (0,)), ((), ())), precision=lax.Precision.HIGHEST)
    factor = jnp.linalg.cholesky(gram_matrix)
    return jax.scipy.linalg.solve_triangular(factor, partial_value.T, lower=True).T

def reference(images, cotangent, conv_weight, conv_bias, norm_gain, norm_bias, expand_weight, expand_bias, reduce_weight, layer_scale, right_first, right_second):
    devices = N_OUTER * N_INNER
    groups = devices // 8
    image_blocks = images.reshape((groups, -1) + images.shape[1:])
    grad_blocks = cotangent.reshape((groups, -1) + cotangent.shape[1:])
    params = (conv_weight, conv_bias, norm_gain, norm_bias, expand_weight, expand_bias, reduce_weight, layer_scale)

    def first_pass(carry, blocks):
        normed, activated, out_grad, hid_grad = local_rows(blocks[0], blocks[1], *params)
        return ((carry[0] + project(normed, hid_grad, right_first), carry[1] + project(activated, out_grad, right_second)), None)
    start = (jnp.zeros((D, RANK), jnp.float32), jnp.zeros((FF, RANK), jnp.float32))
    (p_first, p_second), _ = lax.scan(first_pass, start, (image_blocks, grad_blocks))
    basis_first = orthonormal(p_first)
    basis_second = orthonormal(p_second)

    def second_pass(carry, blocks):
        normed, activated, out_grad, hid_grad = local_rows(blocks[0], blocks[1], *params)
        return ((carry[0] + back_project(normed, hid_grad, basis_first), carry[1] + back_project(activated, out_grad, basis_second)), None)
    start_two = (jnp.zeros((FF, RANK), jnp.float32), jnp.zeros((D, RANK), jnp.float32))
    (next_first, next_second), _ = lax.scan(second_pass, start_two, (image_blocks, grad_blocks))
    scale = jnp.float32(1.0) / devices
    return (next_first * scale, next_second * scale)
```

```python
import jax
import jax.numpy as jnp
from jax import lax
from jax.sharding import PartitionSpec as P


def depthwise(images, conv_weight, conv_bias):
    kernel = conv_weight.shape[0]
    margin = kernel // 2
    extent = images.shape[1]
    widened = jnp.pad(
        images.astype(jnp.float32), ((0, 0), (margin, margin), (margin, margin), (0, 0))
    )
    summed = jnp.zeros(images.shape, jnp.float32) + conv_bias
    for tap_row in range(kernel):
        for tap_col in range(kernel):
            summed = (
                summed
                + widened[:, tap_row : tap_row + extent, tap_col : tap_col + extent, :]
                * conv_weight[tap_row, tap_col]
            )
    return summed


def layer_norm(values, norm_gain, norm_bias):
    center = jnp.mean(values, axis=-1, keepdims=True)
    spread = jnp.mean((values - center) ** 2, axis=-1, keepdims=True)
    return ((values - center) * lax.rsqrt(spread + 1e-06) * norm_gain + norm_bias).astype(
        jnp.bfloat16
    )


def gelu_slope(hidden):
    return (
        0.5 * (1.0 + lax.erf(hidden * 0.7071067811865476))
        + hidden * jnp.exp(-0.5 * hidden * hidden) * 0.3989422804014327
    )


def project(rows_left, rows_right, right):
    thin = jnp.dot(
        rows_right, right.astype(jnp.bfloat16), preferred_element_type=jnp.float32
    ).astype(jnp.bfloat16)
    return lax.dot_general(
        rows_left, thin, (((0,), (0,)), ((), ())), preferred_element_type=jnp.float32
    )


def back_project(rows_left, rows_right, basis):
    rounded = basis.astype(jnp.bfloat16)
    thin = jnp.dot(rows_left, rounded, preferred_element_type=jnp.float32).astype(jnp.bfloat16)
    return lax.dot_general(
        rows_right, thin, (((0,), (0,)), ((), ())), preferred_element_type=jnp.float32
    )


def gram_of(partial_value):
    return lax.dot_general(
        partial_value, partial_value, (((0,), (0,)), ((), ())), precision=lax.Precision.HIGHEST
    )


def apply_factor(gram_matrix, partial_value):
    factor = jnp.linalg.cholesky(gram_matrix)
    return jax.scipy.linalg.solve_triangular(factor, partial_value.T, lower=True).T


def digits(size):
    found = []
    factor = 2
    while size > 1:
        while size % factor == 0:
            found.append(factor)
            size //= factor
        factor += 1
    return found


def plan(n_outer, n_inner):
    steps = []
    stride = 1
    for size in (n_inner, n_outer):
        for radix in digits(size):
            steps.append((stride, radix))
            stride *= radix
    return steps


def linear_index():
    return lax.axis_index("outer") * lax.axis_size("inner") + lax.axis_index("inner")


def shifted(value, count, stride, radix, amount):
    perm = []
    for source in range(count):
        digit = (source // stride) % radix
        target = source + ((digit + amount) % radix - digit) * stride
        perm.append((source, target))
    return lax.ppermute(value, ("outer", "inner"), perm)


def step_sum(value, count, stride, radix, mirror):
    sent = value.astype(jnp.bfloat16)
    if radix == 2:
        mask = stride | mirror
        perm = [(source, source ^ mask) for source in range(count)]
        got = lax.ppermute(sent, ("outer", "inner"), perm)
        return sent.astype(jnp.float32) + got.astype(jnp.float32)
    mine = (linear_index() // stride) % radix
    parts = jnp.stack([sent] + [shifted(sent, count, stride, radix, k) for k in range(1, radix)])
    total = jnp.zeros(value.shape, jnp.float32)
    for owner in range(radix):
        total = total + parts[(mine - owner) % radix].astype(jnp.float32)
    return total


def exchange_sum(stacked):
    n_outer, n_inner = lax.axis_size("outer"), lax.axis_size("inner")
    count = n_outer * n_inner
    steps = plan(n_outer, n_inner)
    paired = bool(steps) and steps[0][1] == 2 and stacked.shape[0] % 32 == 0
    value = stacked
    if paired:
        half = stacked.shape[0] // 2
        mine = linear_index() % 2
        pair = [(source, source ^ 1) for source in range(count)]
        sent = stacked.astype(jnp.bfloat16)
        keep = lax.dynamic_slice_in_dim(sent, mine * half, half, 0)
        give = lax.dynamic_slice_in_dim(sent, (1 - mine) * half, half, 0)
        got = lax.ppermute(give, ("outer", "inner"), pair)
        value = keep.astype(jnp.float32) + got.astype(jnp.float32)
        steps = steps[1:]
    for place, (stride, radix) in enumerate(steps):
        before = steps[place - 1] if place else None
        last = place == len(steps) - 1 and radix == 2 and before is not None
        mirror = before[0] if last and before[1] == 2 and stride > n_inner else 0
        value = step_sum(value, count, stride, radix, mirror)
    value = value.astype(jnp.bfloat16)
    if paired:
        other = lax.ppermute(value, ("outer", "inner"), pair)
        low = jnp.where(mine == 0, value, other)
        high = jnp.where(mine == 0, other, value)
        value = jnp.concatenate([low, high], axis=0)
    return value.astype(jnp.float32)


def sum_layers(first, second):
    total = exchange_sum(jnp.concatenate([first.T, second.T], axis=1))
    cut = first.shape[0]
    return total[:, :cut].T, total[:, cut:].T


def shards(
    images,
    cotangent,
    conv_weight,
    conv_bias,
    norm_gain,
    norm_bias,
    expand_weight,
    expand_bias,
    reduce_weight,
    layer_scale,
    right_first,
    right_second,
):
    count = lax.axis_size("outer") * lax.axis_size("inner")
    scale = jnp.float32(1.0) / count
    width = images.shape[-1]
    conv_out = depthwise(images, conv_weight, conv_bias).reshape((-1, width))
    normed = layer_norm(conv_out, norm_gain, norm_bias)
    hidden = jnp.dot(normed, expand_weight, preferred_element_type=jnp.float32) + expand_bias
    activated = jax.nn.gelu(hidden, approximate=False).astype(jnp.bfloat16)
    out_grad = (cotangent.reshape((-1, width)).astype(jnp.float32) * layer_scale).astype(
        jnp.bfloat16
    )
    p_second = project(activated, out_grad, right_second)
    back = lax.dot_general(
        out_grad, reduce_weight, (((1,), (1,)), ((), ())), preferred_element_type=jnp.float32
    )
    hid_grad = (back * gelu_slope(hidden)).astype(jnp.bfloat16)
    p_first = project(normed, hid_grad, right_first)
    p_first, p_second = sum_layers(p_first, p_second)
    basis_first = apply_factor(gram_of(p_first), p_first)
    basis_second = apply_factor(gram_of(p_second), p_second)
    term_first = back_project(normed, hid_grad, basis_first)
    term_second = back_project(activated, out_grad, basis_second)
    next_first, next_second = sum_layers(term_first, term_second)
    return (next_first * scale, next_second * scale)


def solution(mesh):
    in_specs = (
        P(("outer", "inner"), None, None, None),
        P(("outer", "inner"), None, None, None),
        P(),
        P(),
        P(),
        P(),
        P(),
        P(),
        P(),
        P(),
        P(),
        P(),
    )
    out_specs = (P(), P())
    return jax.shard_map(shards, mesh=mesh, in_specs=in_specs, out_specs=out_specs, check_vma=False)
```

```python
import functools

import jax
import jax.numpy as jnp
from jax import lax
from jax.experimental import pallas as pl
from jax.experimental.pallas import tpu as pltpu
from jax.sharding import PartitionSpec as P

LANES = 128
ROW = 16
LEFT = 8
BLOCK = 512


def phase_one(
    mine_ref,
    images_hbm,
    cotangent_hbm,
    taps_hbm,
    conv_bias_ref,
    gain_ref,
    norm_bias_ref,
    expand_hbm,
    expand_bias_ref,
    reduce_hbm,
    layer_scale_ref,
    first_hbm,
    second_hbm,
    keep_ref,
    give_ref,
    normed_ref,
    activated_ref,
    grad_ref,
    hid_ref,
    image,
    cot,
    taps,
    wide,
    conv,
    expand,
    reduce,
    first,
    second,
    low,
    high,
    sems,
):
    extent, channels = images_hbm.shape[1], images_hbm.shape[3]
    kernel = taps_hbm.shape[0]
    margin = kernel // 2
    hidden_units = expand_hbm.shape[1]
    blocks = hidden_units // BLOCK
    slabs = channels // LANES
    half = keep_ref.shape[0]

    def copies():
        yield pltpu.make_async_copy(images_hbm.at[0], image, sems.at[0])
        yield pltpu.make_async_copy(taps_hbm, taps, sems.at[1])
        yield pltpu.make_async_copy(cotangent_hbm.at[0], cot, sems.at[2])
        yield pltpu.make_async_copy(second_hbm, second, sems.at[3])
        for j in range(blocks):
            cut = pl.ds(j * BLOCK, BLOCK)
            yield pltpu.make_async_copy(expand_hbm.at[:, cut], expand.at[:, cut], sems.at[5 + 2 * j])
            yield pltpu.make_async_copy(reduce_hbm.at[cut, :], reduce.at[cut, :], sems.at[6 + 2 * j])
            if j == 0:
                yield pltpu.make_async_copy(first_hbm, first, sems.at[4])

    started = list(copies())
    for copy in started:
        copy.start()
    image_copy, taps_copy, cot_copy, second_copy = started[:4]
    rest = started[4:6] + started[7:]
    first_copy = started[6]

    wide[...] = jnp.zeros(wide.shape, jnp.float32)
    image_copy.wait()
    for row in range(extent):
        for slab in range(slabs):
            piece = image[row, :, slab * LANES : (slab + 1) * LANES].astype(jnp.float32)
            wide[slab, margin + row, LEFT : LEFT + extent, :] = piece
    taps_copy.wait()

    pieces = 2 if extent % 2 == 0 else 1
    tall = extent // pieces
    for slab in range(slabs):
        lanes = slice(slab * LANES, (slab + 1) * LANES)
        for piece in range(pieces):
            top = piece * tall
            total = jnp.broadcast_to(
                conv_bias_ref[:, lanes].reshape(1, 1, LANES), (tall, ROW, LANES)
            )
            for col in range(kernel):
                start = LEFT - margin + col
                seen = wide[slab, top : top + tall + kernel - 1, start : start + ROW, :]
                for row in range(kernel):
                    tap = taps[row, col : col + 1, lanes].reshape(1, 1, LANES)
                    total = total + seen[row : row + tall] * tap
            conv[slab, top * ROW : (top + tall) * ROW, :] = total.reshape(tall * ROW, LANES)

    rows = extent * ROW
    added = conv[0]
    for slab in range(1, slabs):
        added = added + conv[slab]
    center = jnp.sum(added, axis=-1, keepdims=True) * (1.0 / channels)
    added = jnp.zeros((rows, LANES), jnp.float32)
    for slab in range(slabs):
        away = conv[slab] - center
        added = added + away * away
    spread = jnp.sum(added, axis=-1, keepdims=True) * (1.0 / channels)
    inverse = lax.rsqrt(spread + 1e-06)
    place = lax.broadcasted_iota(jnp.int32, (rows, LANES), 0)
    real = lax.rem(place, ROW) < extent
    for slab in range(slabs):
        lanes = slice(slab * LANES, (slab + 1) * LANES)
        value = (conv[slab] - center) * inverse * gain_ref[:, lanes] + norm_bias_ref[:, lanes]
        normed_ref[:, lanes] = jnp.where(real, value, 0.0).astype(jnp.bfloat16)

    cot_copy.wait()
    grad_ref[...] = jnp.zeros(grad_ref.shape, jnp.bfloat16)
    for row in range(extent):
        piece = cot[row].astype(jnp.float32) * layer_scale_ref[...]
        grad_ref[row * ROW : row * ROW + extent, :] = piece.astype(jnp.bfloat16)

    second_copy.wait()
    normed = normed_ref[...]
    grad = grad_ref[...]
    thin = jnp.dot(grad, second[...].astype(jnp.bfloat16), preferred_element_type=jnp.float32)
    thin_second = thin.T.astype(jnp.bfloat16)
    first_copy.wait()
    thin = jnp.zeros((rows, first.shape[1]), jnp.float32)
    for j in range(blocks):
        cut = slice(j * BLOCK, (j + 1) * BLOCK)
        rest[2 * j].wait()
        hidden = jnp.dot(normed, expand[:, cut], preferred_element_type=jnp.float32)
        hidden = hidden + expand_bias_ref[:, cut]
        rest[2 * j + 1].wait()
        back = lax.dot_general(
            grad, reduce[cut, :], (((1,), (1,)), ((), ())), preferred_element_type=jnp.float32
        )
        cdf = 0.5 * (1.0 + lax.erf(hidden * 0.7071067811865476))
        slope = cdf + hidden * jnp.exp(-0.5 * hidden * hidden) * 0.3989422804014327
        activated = (hidden * cdf).astype(jnp.bfloat16)
        hid = (back * slope).astype(jnp.bfloat16)
        activated_ref[:, cut] = activated
        hid_ref[:, cut] = hid
        thin = thin + jnp.dot(
            hid, first[cut, :].astype(jnp.bfloat16), preferred_element_type=jnp.float32
        )
        sums = jnp.dot(thin_second, activated, preferred_element_type=jnp.float32)
        spot = slice(channels + j * BLOCK, channels + (j + 1) * BLOCK)
        low[:, spot] = sums[:half]
        high[:, spot] = sums[half:]
    sums = jnp.dot(thin.T.astype(jnp.bfloat16), normed, preferred_element_type=jnp.float32)
    low[:, :channels] = sums[:half]
    high[:, :channels] = sums[half:]
    mine = mine_ref[0]

    @pl.when(mine == 0)
    def _():
        keep_ref[...] = low[...]
        give_ref[...] = high[...].astype(jnp.bfloat16)

    @pl.when(mine != 0)
    def _():
        keep_ref[...] = high[...]
        give_ref[...] = low[...].astype(jnp.bfloat16)


def eliminate(gram_matrix, size):
    wide = 2 * size
    spot = lax.broadcasted_iota(jnp.int32, (size, size), 0)
    across = lax.broadcasted_iota(jnp.int32, (size, size), 1)
    eye = jnp.where(spot == across, 1.0, 0.0).astype(jnp.float32)
    work = jnp.concatenate([gram_matrix, eye], axis=1)
    down = lax.broadcasted_iota(jnp.int32, (size, wide), 0)
    group = 4
    for base in range(0, size, group):
        cols = [
            jnp.broadcast_to(work[:, base + b : base + b + 1], (size, wide)) for b in range(group)
        ]
        rows = [work[base + b : base + b + 1, :] for b in range(group)]
        for b in range(group):
            scale = lax.rsqrt(cols[b][base + b : base + b + 1, :])
            rows[b] = rows[b] * scale
            cols[b] = cols[b] * scale
            for c in range(b + 1, group):
                factor = cols[b][base + c : base + c + 1, :]
                rows[c] = rows[c] - factor * rows[b]
                cols[c] = cols[c] - cols[b] * factor
        change = jnp.zeros((size, wide), jnp.float32)
        for b in range(group):
            change = change + cols[b] * rows[b]
        work = jnp.where(down >= base + group, work - change, work)
        for b in range(group):
            work = jnp.where(down == base + b, rows[b], work)
    return work[:, size:]


def phase_two(
    mine_ref, value_ref, other_ref, normed_ref, activated_ref, grad_ref, hid_ref, keep_ref, give_ref
):
    channels = normed_ref.shape[1]
    half = value_ref.shape[0]
    mine = mine_ref[0]
    value = value_ref[...]
    other = other_ref[...]
    low = jnp.where(mine == 0, value, other)
    high = jnp.where(mine == 0, other, value)
    both = jnp.concatenate([low, high], axis=0)
    nt = (((1,), (1,)), ((), ()))
    bases = []
    for part in (both[:, :channels], both[:, channels:]):
        gram_matrix = lax.dot_general(part, part, nt, preferred_element_type=jnp.float32)
        inverse = eliminate(gram_matrix, 2 * half)
        coarse = inverse.astype(jnp.bfloat16)
        fine = (inverse - coarse.astype(jnp.float32)).astype(jnp.bfloat16)
        basis = jnp.dot(coarse, part, preferred_element_type=jnp.float32)
        basis = basis + jnp.dot(fine, part, preferred_element_type=jnp.float32)
        bases.append(basis.astype(jnp.bfloat16))
    thin = lax.dot_general(bases[0], normed_ref[...], nt, preferred_element_type=jnp.float32)
    first = jnp.dot(thin.astype(jnp.bfloat16), hid_ref[...], preferred_element_type=jnp.float32)
    thin = lax.dot_general(bases[1], activated_ref[...], nt, preferred_element_type=jnp.float32)
    second = jnp.dot(thin.astype(jnp.bfloat16), grad_ref[...], preferred_element_type=jnp.float32)
    for piece, spot in ((second, slice(0, channels)), (first, slice(channels, None))):
        keep_ref[:, spot] = jnp.where(mine == 0, piece[:half], piece[half:])
        give_ref[:, spot] = jnp.where(mine == 0, piece[half:], piece[:half]).astype(jnp.bfloat16)


def digits(size):
    found = []
    factor = 2
    while size > 1:
        while size % factor == 0:
            found.append(factor)
            size //= factor
        factor += 1
    return found


def plan(n_outer, n_inner):
    steps = []
    stride = 1
    for size in (n_inner, n_outer):
        for radix in digits(size):
            steps.append((stride, radix))
            stride *= radix
    return steps


def linear_index():
    return lax.axis_index("outer") * lax.axis_size("inner") + lax.axis_index("inner")


def shifted(value, count, stride, radix, amount):
    perm = []
    for source in range(count):
        digit = (source // stride) % radix
        target = source + ((digit + amount) % radix - digit) * stride
        perm.append((source, target))
    return lax.ppermute(value, ("outer", "inner"), perm)


def step_sum(value, count, stride, radix, mirror):
    sent = value.astype(jnp.bfloat16)
    if radix == 2:
        mask = stride | mirror
        perm = [(source, source ^ mask) for source in range(count)]
        got = lax.ppermute(sent, ("outer", "inner"), perm)
        return sent.astype(jnp.float32) + got.astype(jnp.float32)
    mine = (linear_index() // stride) % radix
    parts = jnp.stack([sent] + [shifted(sent, count, stride, radix, k) for k in range(1, radix)])
    total = jnp.zeros(value.shape, jnp.float32)
    for owner in range(radix):
        total = total + parts[(mine - owner) % radix].astype(jnp.float32)
    return total


def pair_perm(count):
    return [(source, source ^ 1) for source in range(count)]


def exchange(keep, give, mine):
    n_outer, n_inner = lax.axis_size("outer"), lax.axis_size("inner")
    count = n_outer * n_inner
    steps = plan(n_outer, n_inner)[1:]
    got = lax.ppermute(give, ("outer", "inner"), pair_perm(count))
    value = keep + got.astype(jnp.float32)
    for place, (stride, radix) in enumerate(steps):
        before = steps[place - 1] if place else None
        last = place == len(steps) - 1 and radix == 2 and before is not None
        mirror = before[0] if last and before[1] == 2 and stride > n_inner else 0
        value = step_sum(value, count, stride, radix, mirror)
    value = value.astype(jnp.bfloat16)
    other = lax.ppermute(value, ("outer", "inner"), pair_perm(count))
    return value, other


VMEM = pl.BlockSpec(memory_space=pltpu.VMEM)
ANY = pl.BlockSpec(memory_space=pl.ANY)
SMEM = pl.BlockSpec(memory_space=pltpu.SMEM)


def shards(
    images,
    cotangent,
    conv_weight,
    conv_bias,
    norm_gain,
    norm_bias,
    expand_weight,
    expand_bias,
    reduce_weight,
    layer_scale,
    right_first,
    right_second,
):
    count = lax.axis_size("outer") * lax.axis_size("inner")
    scale = jnp.float32(1.0) / count
    extent, width = images.shape[1], images.shape[3]
    kernel = conv_weight.shape[0]
    hidden_units = expand_weight.shape[1]
    rank = right_first.shape[1]
    rows, half, total = extent * ROW, rank // 2, width + hidden_units
    slabs = width // LANES
    bf16, f32 = jnp.bfloat16, jnp.float32
    mine = (linear_index() % 2).astype(jnp.int32).reshape(1)
    keep, give, normed, activated, grad, hid = pl.pallas_call(
        phase_one,
        out_shape=(
            jax.ShapeDtypeStruct((half, total), f32),
            jax.ShapeDtypeStruct((half, total), bf16),
            jax.ShapeDtypeStruct((rows, width), bf16),
            jax.ShapeDtypeStruct((rows, hidden_units), bf16),
            jax.ShapeDtypeStruct((rows, width), bf16),
            jax.ShapeDtypeStruct((rows, hidden_units), bf16),
        ),
        in_specs=[SMEM, ANY, ANY, ANY, VMEM, VMEM, VMEM, ANY, VMEM, ANY, VMEM, ANY, ANY],
        out_specs=(VMEM,) * 6,
        scratch_shapes=[
            pltpu.VMEM(images.shape[1:], bf16),
            pltpu.VMEM(images.shape[1:], bf16),
            pltpu.VMEM(conv_weight.shape, f32),
            pltpu.VMEM((slabs, extent + kernel - 1, 2 * ROW, LANES), f32),
            pltpu.VMEM((slabs, rows, LANES), f32),
            pltpu.VMEM(expand_weight.shape, bf16),
            pltpu.VMEM(reduce_weight.shape, bf16),
            pltpu.VMEM(right_first.shape, f32),
            pltpu.VMEM(right_second.shape, f32),
            pltpu.VMEM((half, total), f32),
            pltpu.VMEM((half, total), f32),
            pltpu.SemaphoreType.DMA((5 + 2 * (hidden_units // BLOCK),)),
        ],
        compiler_params=pltpu.CompilerParams(vmem_limit_bytes=40 * 1024 * 1024),
        name="phase_one",
    )(
        mine,
        images,
        cotangent,
        conv_weight,
        conv_bias.reshape(1, -1),
        norm_gain.reshape(1, -1),
        norm_bias.reshape(1, -1),
        expand_weight,
        expand_bias.reshape(1, -1),
        reduce_weight,
        layer_scale.reshape(1, -1),
        right_first,
        right_second,
    )
    value, other = exchange(keep, give, mine)
    keep, give = pl.pallas_call(
        phase_two,
        out_shape=(
            jax.ShapeDtypeStruct((half, total), f32),
            jax.ShapeDtypeStruct((half, total), bf16),
        ),
        in_specs=[SMEM] + [VMEM] * 6,
        out_specs=(VMEM, VMEM),
        compiler_params=pltpu.CompilerParams(vmem_limit_bytes=40 * 1024 * 1024),
        name="phase_two",
    )(mine, value, other, normed, activated, grad, hid)
    value, other = exchange(keep, give, mine)
    low = jnp.where(mine[0] == 0, value, other)
    high = jnp.where(mine[0] == 0, other, value)
    both = jnp.concatenate([low, high], axis=0).astype(f32) * scale
    return (both[:, width:].T, both[:, :width].T)


def solution(mesh):
    in_specs = (
        P(("outer", "inner"), None, None, None),
        P(("outer", "inner"), None, None, None),
        P(),
        P(),
        P(),
        P(),
        P(),
        P(),
        P(),
        P(),
        P(),
        P(),
    )
    out_specs = (P(), P())
    return jax.shard_map(shards, mesh=mesh, in_specs=in_specs, out_specs=out_specs, check_vma=False)
```

```python
import functools

import jax
import jax.numpy as jnp
from jax import lax
from jax.experimental import pallas as pl
from jax.experimental.pallas import tpu as pltpu
from jax.sharding import PartitionSpec as P

LANES = 128
ROW = 16
LEFT = 8
BLOCK = 512


def phase_one(
    mine_ref,
    images_hbm,
    cotangent_hbm,
    taps_hbm,
    conv_bias_ref,
    gain_ref,
    norm_bias_ref,
    expand_hbm,
    expand_bias_ref,
    reduce_hbm,
    layer_scale_ref,
    first_hbm,
    second_hbm,
    keep_ref,
    give_ref,
    normed_ref,
    activated_ref,
    grad_ref,
    hid_ref,
    image,
    cot,
    taps,
    wide,
    conv,
    expand,
    reduce,
    first,
    second,
    low,
    high,
    sems,
):
    extent, channels = images_hbm.shape[1], images_hbm.shape[3]
    kernel = taps_hbm.shape[0]
    margin = kernel // 2
    hidden_units = expand_hbm.shape[1]
    blocks = hidden_units // BLOCK
    slabs = channels // LANES
    half = keep_ref.shape[0]

    def copies():
        yield pltpu.make_async_copy(images_hbm.at[0], image, sems.at[0])
        yield pltpu.make_async_copy(taps_hbm, taps, sems.at[1])
        yield pltpu.make_async_copy(cotangent_hbm.at[0], cot, sems.at[2])
        yield pltpu.make_async_copy(second_hbm, second, sems.at[3])
        for j in range(blocks):
            cut = pl.ds(j * BLOCK, BLOCK)
            yield pltpu.make_async_copy(expand_hbm.at[:, cut], expand.at[:, cut], sems.at[5 + 2 * j])
            yield pltpu.make_async_copy(reduce_hbm.at[cut, :], reduce.at[cut, :], sems.at[6 + 2 * j])
            if j == 0:
                yield pltpu.make_async_copy(first_hbm, first, sems.at[4])

    started = list(copies())
    for copy in started:
        copy.start()
    image_copy, taps_copy, cot_copy, second_copy = started[:4]
    rest = started[4:6] + started[7:]
    first_copy = started[6]

    wide[...] = jnp.zeros(wide.shape, jnp.float32)
    image_copy.wait()
    for row in range(extent):
        for slab in range(slabs):
            piece = image[row, :, slab * LANES : (slab + 1) * LANES].astype(jnp.float32)
            wide[slab, margin + row, LEFT : LEFT + extent, :] = piece
    taps_copy.wait()

    pieces = 2 if extent % 2 == 0 else 1
    tall = extent // pieces
    for slab in range(slabs):
        lanes = slice(slab * LANES, (slab + 1) * LANES)
        for piece in range(pieces):
            top = piece * tall
            total = jnp.broadcast_to(
                conv_bias_ref[:, lanes].reshape(1, 1, LANES), (tall, ROW, LANES)
            )
            for col in range(kernel):
                start = LEFT - margin + col
                seen = wide[slab, top : top + tall + kernel - 1, start : start + ROW, :]
                for row in range(kernel):
                    tap = taps[row, col : col + 1, lanes].reshape(1, 1, LANES)
                    total = total + seen[row : row + tall] * tap
            conv[slab, top * ROW : (top + tall) * ROW, :] = total.reshape(tall * ROW, LANES)

    rows = extent * ROW
    added = conv[0]
    for slab in range(1, slabs):
        added = added + conv[slab]
    center = jnp.sum(added, axis=-1, keepdims=True) * (1.0 / channels)
    added = jnp.zeros((rows, LANES), jnp.float32)
    for slab in range(slabs):
        away = conv[slab] - center
        added = added + away * away
    spread = jnp.sum(added, axis=-1, keepdims=True) * (1.0 / channels)
    inverse = lax.rsqrt(spread + 1e-06)
    place = lax.broadcasted_iota(jnp.int32, (rows, LANES), 0)
    real = lax.rem(place, ROW) < extent
    for slab in range(slabs):
        lanes = slice(slab * LANES, (slab + 1) * LANES)
        value = (conv[slab] - center) * inverse * gain_ref[:, lanes] + norm_bias_ref[:, lanes]
        normed_ref[:, lanes] = jnp.where(real, value, 0.0).astype(jnp.bfloat16)

    cot_copy.wait()
    grad_ref[...] = jnp.zeros(grad_ref.shape, jnp.bfloat16)
    for row in range(extent):
        piece = cot[row].astype(jnp.float32) * layer_scale_ref[...]
        grad_ref[row * ROW : row * ROW + extent, :] = piece.astype(jnp.bfloat16)

    second_copy.wait()
    normed = normed_ref[...]
    grad = grad_ref[...]
    thin = jnp.dot(grad, second[...].astype(jnp.bfloat16), preferred_element_type=jnp.float32)
    thin_second = thin.T.astype(jnp.bfloat16)
    first_copy.wait()
    thin = jnp.zeros((rows, first.shape[1]), jnp.float32)
    for j in range(blocks):
        cut = slice(j * BLOCK, (j + 1) * BLOCK)
        rest[2 * j].wait()
        hidden = jnp.dot(normed, expand[:, cut], preferred_element_type=jnp.float32)
        hidden = hidden + expand_bias_ref[:, cut]
        rest[2 * j + 1].wait()
        back = lax.dot_general(
            grad, reduce[cut, :], (((1,), (1,)), ((), ())), preferred_element_type=jnp.float32
        )
        cdf = 0.5 * (1.0 + lax.erf(hidden * 0.7071067811865476))
        slope = cdf + hidden * jnp.exp(-0.5 * hidden * hidden) * 0.3989422804014327
        activated = (hidden * cdf).astype(jnp.bfloat16)
        hid = (back * slope).astype(jnp.bfloat16)
        activated_ref[:, cut] = activated
        hid_ref[:, cut] = hid
        thin = thin + jnp.dot(
            hid, first[cut, :].astype(jnp.bfloat16), preferred_element_type=jnp.float32
        )
        sums = jnp.dot(thin_second, activated, preferred_element_type=jnp.float32)
        spot = slice(channels + j * BLOCK, channels + (j + 1) * BLOCK)
        low[:, spot] = sums[:half]
        high[:, spot] = sums[half:]
    sums = jnp.dot(thin.T.astype(jnp.bfloat16), normed, preferred_element_type=jnp.float32)
    low[:, :channels] = sums[:half]
    high[:, :channels] = sums[half:]
    mine = mine_ref[0]

    @pl.when(mine == 0)
    def _():
        keep_ref[...] = low[...]
        give_ref[...] = high[...].astype(jnp.bfloat16)

    @pl.when(mine != 0)
    def _():
        keep_ref[...] = high[...]
        give_ref[...] = low[...].astype(jnp.bfloat16)


def eliminate(gram_matrix, size):
    wide = 2 * size
    spot = lax.broadcasted_iota(jnp.int32, (size, size), 0)
    across = lax.broadcasted_iota(jnp.int32, (size, size), 1)
    eye = jnp.where(spot == across, 1.0, 0.0).astype(jnp.float32)
    work = jnp.concatenate([gram_matrix, eye], axis=1)
    down = lax.broadcasted_iota(jnp.int32, (size, wide), 0)
    group = 4
    for base in range(0, size, group):
        cols = [
            jnp.broadcast_to(work[:, base + b : base + b + 1], (size, wide)) for b in range(group)
        ]
        rows = [work[base + b : base + b + 1, :] for b in range(group)]
        for b in range(group):
            scale = lax.rsqrt(cols[b][base + b : base + b + 1, :])
            rows[b] = rows[b] * scale
            cols[b] = cols[b] * scale
            for c in range(b + 1, group):
                factor = cols[b][base + c : base + c + 1, :]
                rows[c] = rows[c] - factor * rows[b]
                cols[c] = cols[c] - cols[b] * factor
        change = jnp.zeros((size, wide), jnp.float32)
        for b in range(group):
            change = change + cols[b] * rows[b]
        work = jnp.where(down >= base + group, work - change, work)
        for b in range(group):
            work = jnp.where(down == base + b, rows[b], work)
    return work[:, size:]


def phase_two(
    mine_ref, value_ref, other_ref, normed_ref, activated_ref, grad_ref, hid_ref, keep_ref, give_ref
):
    channels = normed_ref.shape[1]
    half = value_ref.shape[0]
    mine = mine_ref[0]
    value = value_ref[...]
    other = other_ref[...]
    low = jnp.where(mine == 0, value, other)
    high = jnp.where(mine == 0, other, value)
    both = jnp.concatenate([low, high], axis=0)
    nt = (((1,), (1,)), ((), ()))
    bases = []
    for part in (both[:, :channels], both[:, channels:]):
        gram_matrix = lax.dot_general(part, part, nt, preferred_element_type=jnp.float32)
        inverse = eliminate(gram_matrix, 2 * half)
        coarse = inverse.astype(jnp.bfloat16)
        fine = (inverse - coarse.astype(jnp.float32)).astype(jnp.bfloat16)
        basis = jnp.dot(coarse, part, preferred_element_type=jnp.float32)
        basis = basis + jnp.dot(fine, part, preferred_element_type=jnp.float32)
        bases.append(basis.astype(jnp.bfloat16))
    thin = lax.dot_general(bases[0], normed_ref[...], nt, preferred_element_type=jnp.float32)
    first = jnp.dot(thin.astype(jnp.bfloat16), hid_ref[...], preferred_element_type=jnp.float32)
    thin = lax.dot_general(bases[1], activated_ref[...], nt, preferred_element_type=jnp.float32)
    second = jnp.dot(thin.astype(jnp.bfloat16), grad_ref[...], preferred_element_type=jnp.float32)
    for piece, spot in ((second, slice(0, channels)), (first, slice(channels, None))):
        keep_ref[:, spot] = jnp.where(mine == 0, piece[:half], piece[half:])
        give_ref[:, spot] = jnp.where(mine == 0, piece[half:], piece[:half]).astype(jnp.bfloat16)


def digits(size):
    found = []
    factor = 2
    while size > 1:
        while size % factor == 0:
            found.append(factor)
            size //= factor
        factor += 1
    return found


def plan(n_outer, n_inner):
    steps = []
    stride = 1
    for size in (n_inner, n_outer):
        for radix in digits(size):
            steps.append((stride, radix))
            stride *= radix
    return steps


def linear_index():
    return lax.axis_index("outer") * lax.axis_size("inner") + lax.axis_index("inner")


def shifted(value, count, stride, radix, amount):
    perm = []
    for source in range(count):
        digit = (source // stride) % radix
        target = source + ((digit + amount) % radix - digit) * stride
        perm.append((source, target))
    return lax.ppermute(value, ("outer", "inner"), perm)


def turn(value, count, stride, radix):
    sent = value.astype(jnp.bfloat16)
    mine = (linear_index() // stride) % radix
    parts = jnp.stack([sent] + [shifted(sent, count, stride, radix, k) for k in range(1, radix)])
    total = jnp.zeros(value.shape, jnp.float32)
    for owner in range(radix):
        total = total + parts[(mine - owner) % radix].astype(jnp.float32)
    return total


def swap_stages(steps):
    masks = [stride for stride, radix in steps if radix == 2]
    even = len(masks) // 2 * 2
    return [masks[k : k + 2] for k in range(0, even, 2)], [[mask] for mask in masks[even:]]


def swap_sum(value, count, orders):
    sent = value.astype(jnp.bfloat16)

    def partner(pick):
        masks = []
        for stage in orders:
            mask = 0
            for k in pick:
                mask ^= stage[k]
            masks.append(mask)
        perm = [(source, source ^ masks[source % 2]) for source in range(count)]
        return lax.ppermute(sent, ("outer", "inner"), perm).astype(jnp.float32)

    if len(orders[0]) == 1:
        return sent.astype(jnp.float32) + partner((0,))
    near, far, both = partner((0,)), partner((1,)), partner((0, 1))
    return (sent.astype(jnp.float32) + near) + (far + both)


def pair_perm(count):
    return [(source, source ^ 1) for source in range(count)]


def exchange(keep, give, mine):
    n_outer, n_inner = lax.axis_size("outer"), lax.axis_size("inner")
    count = n_outer * n_inner
    steps = plan(n_outer, n_inner)[1:]
    got = lax.ppermute(give, ("outer", "inner"), pair_perm(count))
    value = keep + got.astype(jnp.float32)
    quads, singles = swap_stages(steps)
    cut = len(quads) // 2
    for even, odd in zip(quads + singles, quads[cut:] + quads[:cut] + singles):
        value = swap_sum(value, count, (even, odd))
    for stride, radix in steps:
        if radix != 2:
            value = turn(value, count, stride, radix)
    value = value.astype(jnp.bfloat16)
    other = lax.ppermute(value, ("outer", "inner"), pair_perm(count))
    return value, other


VMEM = pl.BlockSpec(memory_space=pltpu.VMEM)
ANY = pl.BlockSpec(memory_space=pl.ANY)
SMEM = pl.BlockSpec(memory_space=pltpu.SMEM)


def shards(
    images,
    cotangent,
    conv_weight,
    conv_bias,
    norm_gain,
    norm_bias,
    expand_weight,
    expand_bias,
    reduce_weight,
    layer_scale,
    right_first,
    right_second,
):
    count = lax.axis_size("outer") * lax.axis_size("inner")
    scale = jnp.float32(1.0) / count
    extent, width = images.shape[1], images.shape[3]
    kernel = conv_weight.shape[0]
    hidden_units = expand_weight.shape[1]
    rank = right_first.shape[1]
    rows, half, total = extent * ROW, rank // 2, width + hidden_units
    slabs = width // LANES
    bf16, f32 = jnp.bfloat16, jnp.float32
    mine = (linear_index() % 2).astype(jnp.int32).reshape(1)
    keep, give, normed, activated, grad, hid = pl.pallas_call(
        phase_one,
        out_shape=(
            jax.ShapeDtypeStruct((half, total), f32),
            jax.ShapeDtypeStruct((half, total), bf16),
            jax.ShapeDtypeStruct((rows, width), bf16),
            jax.ShapeDtypeStruct((rows, hidden_units), bf16),
            jax.ShapeDtypeStruct((rows, width), bf16),
            jax.ShapeDtypeStruct((rows, hidden_units), bf16),
        ),
        in_specs=[SMEM, ANY, ANY, ANY, VMEM, VMEM, VMEM, ANY, VMEM, ANY, VMEM, ANY, ANY],
        out_specs=(VMEM,) * 6,
        scratch_shapes=[
            pltpu.VMEM(images.shape[1:], bf16),
            pltpu.VMEM(images.shape[1:], bf16),
            pltpu.VMEM(conv_weight.shape, f32),
            pltpu.VMEM((slabs, extent + kernel - 1, 2 * ROW, LANES), f32),
            pltpu.VMEM((slabs, rows, LANES), f32),
            pltpu.VMEM(expand_weight.shape, bf16),
            pltpu.VMEM(reduce_weight.shape, bf16),
            pltpu.VMEM(right_first.shape, f32),
            pltpu.VMEM(right_second.shape, f32),
            pltpu.VMEM((half, total), f32),
            pltpu.VMEM((half, total), f32),
            pltpu.SemaphoreType.DMA((5 + 2 * (hidden_units // BLOCK),)),
        ],
        compiler_params=pltpu.CompilerParams(vmem_limit_bytes=40 * 1024 * 1024),
        name="phase_one",
    )(
        mine,
        images,
        cotangent,
        conv_weight,
        conv_bias.reshape(1, -1),
        norm_gain.reshape(1, -1),
        norm_bias.reshape(1, -1),
        expand_weight,
        expand_bias.reshape(1, -1),
        reduce_weight,
        layer_scale.reshape(1, -1),
        right_first,
        right_second,
    )
    value, other = exchange(keep, give, mine)
    keep, give = pl.pallas_call(
        phase_two,
        out_shape=(
            jax.ShapeDtypeStruct((half, total), f32),
            jax.ShapeDtypeStruct((half, total), bf16),
        ),
        in_specs=[SMEM] + [VMEM] * 6,
        out_specs=(VMEM, VMEM),
        compiler_params=pltpu.CompilerParams(vmem_limit_bytes=40 * 1024 * 1024),
        name="phase_two",
    )(mine, value, other, normed, activated, grad, hid)
    value, other = exchange(keep, give, mine)
    low = jnp.where(mine[0] == 0, value, other)
    high = jnp.where(mine[0] == 0, other, value)
    both = jnp.concatenate([low, high], axis=0).astype(f32) * scale
    return (both[:, width:].T, both[:, :width].T)


def solution(mesh):
    in_specs = (
        P(("outer", "inner"), None, None, None),
        P(("outer", "inner"), None, None, None),
        P(),
        P(),
        P(),
        P(),
        P(),
        P(),
        P(),
        P(),
        P(),
        P(),
    )
    out_specs = (P(), P())
    return jax.shard_map(shards, mesh=mesh, in_specs=in_specs, out_specs=out_specs, check_vma=False)
```

```python
import functools

import jax
import jax.numpy as jnp
from jax import lax
from jax.experimental import pallas as pl
from jax.experimental.pallas import tpu as pltpu
from jax.sharding import PartitionSpec as P

LANES = 128
ROW = 16
LEFT = 8
BLOCK = 512


def phase_one(
    mine_ref,
    images_hbm,
    cotangent_hbm,
    taps_hbm,
    conv_bias_hbm,
    gain_hbm,
    norm_bias_hbm,
    expand_hbm,
    expand_bias_hbm,
    reduce_hbm,
    layer_scale_hbm,
    first_hbm,
    second_hbm,
    keep_ref,
    give_ref,
    normed_ref,
    activated_ref,
    grad_ref,
    hid_ref,
    image,
    cot,
    taps,
    conv_bias,
    gain,
    norm_bias,
    layer_scale,
    expand_bias,
    wide,
    conv,
    expand,
    reduce,
    back,
    first,
    second,
    low,
    high,
    sems,
    block_sems,
):
    extent, channels = images_hbm.shape[1], images_hbm.shape[3]
    kernel = taps_hbm.shape[0]
    margin = kernel // 2
    hidden_units = expand_hbm.shape[1]
    blocks = hidden_units // BLOCK
    slabs = channels // LANES
    half = keep_ref.shape[0]
    rows = extent * ROW
    nt = (((1,), (1,)), ((), ()))

    pairs = [
        (images_hbm.at[0], image),
        (taps_hbm, taps),
        (cotangent_hbm.at[0], cot),
        (layer_scale_hbm, layer_scale),
        (conv_bias_hbm, conv_bias),
        (gain_hbm, gain),
        (norm_bias_hbm, norm_bias),
        (expand_bias_hbm, expand_bias),
        (second_hbm, second),
        (first_hbm, first),
        (expand_hbm, expand),
    ]
    copies = [pltpu.make_async_copy(src, dst, sems.at[k]) for k, (src, dst) in enumerate(pairs)]

    def reduce_copy(j):
        cut = pl.ds(pl.multiple_of(j * BLOCK, BLOCK), BLOCK)
        return pltpu.make_async_copy(reduce_hbm.at[cut, :], reduce.at[cut, :], block_sems.at[j])

    for copy in copies[:5]:
        copy.start()
    for j in range(blocks):
        reduce_copy(j).start()
    for copy in copies[5:]:
        copy.start()

    wide[...] = jnp.zeros(wide.shape, jnp.float32)
    grad_ref[...] = jnp.zeros(grad_ref.shape, jnp.bfloat16)
    copies[0].wait()
    for row in range(extent):
        for slab in range(slabs):
            piece = image[row, :, slab * LANES : (slab + 1) * LANES].astype(jnp.float32)
            wide[slab, margin + row, LEFT : LEFT + extent, :] = piece
    copies[2].wait()
    copies[3].wait()
    for row in range(extent):
        piece = cot[row].astype(jnp.float32) * layer_scale[...].reshape(1, channels)
        grad_ref[row * ROW : row * ROW + extent, :] = piece.astype(jnp.bfloat16)
    copies[1].wait()
    copies[4].wait()

    def conv_tile(slab, top, tall):
        lanes = pl.ds(pl.multiple_of(slab * LANES, LANES), LANES)
        total = jnp.broadcast_to(conv_bias[lanes].reshape(1, 1, LANES), (tall, ROW, LANES))
        for col in range(kernel):
            start = LEFT - margin + col
            seen = wide[slab, pl.ds(top, tall + kernel - 1), start : start + ROW, :]
            for row in range(kernel):
                tap = taps[row, col : col + 1, lanes].reshape(1, 1, LANES)
                total = total + seen[row : row + tall] * tap
        spot = pl.ds(pl.multiple_of(top * ROW, ROW), tall * ROW)
        conv[slab, spot, :] = total.reshape(tall * ROW, LANES)

    TALL = 7
    tiles = extent // TALL

    def conv_step(step, _):
        conv_tile(step // tiles, (step % tiles) * TALL, TALL)
        return 0

    def back_block(j):
        reduce_copy(j).wait()
        cut = pl.ds(pl.multiple_of(j * BLOCK, BLOCK), BLOCK)
        back[:, cut] = lax.dot_general(
            grad_ref[...], reduce[cut, :], nt, preferred_element_type=jnp.float32
        )

    if True:
        per = slabs * tiles // blocks

        def both_step(j, _):
            back_block(j)
            for k in range(per):
                step = j * per + k
                conv_tile(step // tiles, (step % tiles) * TALL, TALL)
            return 0

        lax.fori_loop(0, blocks, both_step, 0)
    else:
        lax.fori_loop(0, slabs * tiles, conv_step, 0)

    added = conv[0]
    for slab in range(1, slabs):
        added = added + conv[slab]
    center = jnp.sum(added, axis=-1, keepdims=True) * (1.0 / channels)
    added = jnp.zeros((rows, LANES), jnp.float32)
    for slab in range(slabs):
        away = conv[slab] - center
        added = added + away * away
    spread = jnp.sum(added, axis=-1, keepdims=True) * (1.0 / channels)
    inverse = lax.rsqrt(spread + 1e-06)
    place = lax.broadcasted_iota(jnp.int32, (rows, LANES), 0)
    real = lax.rem(place, ROW) < extent
    for copy in copies[5:]:
        copy.wait()
    for slab in range(slabs):
        lanes = slice(slab * LANES, (slab + 1) * LANES)
        value = (conv[slab] - center) * inverse * gain[lanes].reshape(1, LANES) + norm_bias[lanes].reshape(1, LANES)
        normed_ref[:, lanes] = jnp.where(real, value, 0.0).astype(jnp.bfloat16)

    normed = normed_ref[...]
    thin_second = lax.dot_general(
        second[...].astype(jnp.bfloat16), grad_ref[...], nt, preferred_element_type=jnp.float32
    ).astype(jnp.bfloat16)
    thin = jnp.zeros((first.shape[0], rows), jnp.float32)
    if False:
        for j in range(blocks):
            reduce_copy(j).wait()
    for j in range(blocks):
        cut = slice(j * BLOCK, (j + 1) * BLOCK)
        hidden = jnp.dot(normed, expand[:, cut], preferred_element_type=jnp.float32)
        hidden = hidden + expand_bias[cut].reshape(1, BLOCK)
        if True:
            pulled = back[:, cut]
        else:
            pulled = lax.dot_general(
                grad_ref[...], reduce[cut, :], nt, preferred_element_type=jnp.float32
            )
        cdf = 0.5 * (1.0 + lax.erf(hidden * 0.7071067811865476))
        slope = cdf + hidden * jnp.exp(-0.5 * hidden * hidden) * 0.3989422804014327
        activated = (hidden * cdf).astype(jnp.bfloat16)
        hid = (pulled * slope).astype(jnp.bfloat16)
        activated_ref[:, cut] = activated
        hid_ref[:, cut] = hid
        thin = thin + lax.dot_general(
            first[:, cut].astype(jnp.bfloat16), hid, nt, preferred_element_type=jnp.float32
        )
        sums = jnp.dot(thin_second, activated, preferred_element_type=jnp.float32)
        spot = slice(channels + j * BLOCK, channels + (j + 1) * BLOCK)
        low[:, spot] = sums[:half]
        high[:, spot] = sums[half:]
    sums = jnp.dot(thin.astype(jnp.bfloat16), normed, preferred_element_type=jnp.float32)
    low[:, :channels] = sums[:half]
    high[:, :channels] = sums[half:]
    mine = mine_ref[0]

    @pl.when(mine == 0)
    def _():
        keep_ref[...] = low[...]
        give_ref[...] = high[...].astype(jnp.bfloat16)

    @pl.when(mine != 0)
    def _():
        keep_ref[...] = high[...]
        give_ref[...] = low[...].astype(jnp.bfloat16)


def eliminate(gram_matrix, size):
    wide = 2 * size
    spot = lax.broadcasted_iota(jnp.int32, (size, size), 0)
    across = lax.broadcasted_iota(jnp.int32, (size, size), 1)
    eye = jnp.where(spot == across, 1.0, 0.0).astype(jnp.float32)
    work = jnp.concatenate([gram_matrix, eye], axis=1)
    down = lax.broadcasted_iota(jnp.int32, (size, wide), 0)
    group = 4
    for base in range(0, size, group):
        cols = [
            jnp.broadcast_to(work[:, base + b : base + b + 1], (size, wide)) for b in range(group)
        ]
        rows = [work[base + b : base + b + 1, :] for b in range(group)]
        for b in range(group):
            scale = lax.rsqrt(cols[b][base + b : base + b + 1, :])
            rows[b] = rows[b] * scale
            cols[b] = cols[b] * scale
            for c in range(b + 1, group):
                factor = cols[b][base + c : base + c + 1, :]
                rows[c] = rows[c] - factor * rows[b]
                cols[c] = cols[c] - cols[b] * factor
        change = jnp.zeros((size, wide), jnp.float32)
        for b in range(group):
            change = change + cols[b] * rows[b]
        work = jnp.where(down >= base + group, work - change, work)
        for b in range(group):
            work = jnp.where(down == base + b, rows[b], work)
    return work[:, size:]


def phase_two(
    mine_ref, value_ref, other_ref, normed_ref, activated_ref, grad_ref, hid_ref, keep_ref, give_ref
):
    channels = normed_ref.shape[1]
    half = value_ref.shape[0]
    mine = mine_ref[0]
    value = value_ref[...]
    other = other_ref[...]
    low = jnp.where(mine == 0, value, other)
    high = jnp.where(mine == 0, other, value)
    both = jnp.concatenate([low, high], axis=0)
    nt = (((1,), (1,)), ((), ()))
    bases = []
    for part in (both[:, :channels], both[:, channels:]):
        gram_matrix = lax.dot_general(part, part, nt, preferred_element_type=jnp.float32)
        inverse = eliminate(gram_matrix, 2 * half)
        coarse = inverse.astype(jnp.bfloat16)
        fine = (inverse - coarse.astype(jnp.float32)).astype(jnp.bfloat16)
        basis = jnp.dot(coarse, part, preferred_element_type=jnp.float32)
        basis = basis + jnp.dot(fine, part, preferred_element_type=jnp.float32)
        bases.append(basis.astype(jnp.bfloat16))
    thin = lax.dot_general(bases[0], normed_ref[...], nt, preferred_element_type=jnp.float32)
    first = jnp.dot(thin.astype(jnp.bfloat16), hid_ref[...], preferred_element_type=jnp.float32)
    thin = lax.dot_general(bases[1], activated_ref[...], nt, preferred_element_type=jnp.float32)
    second = jnp.dot(thin.astype(jnp.bfloat16), grad_ref[...], preferred_element_type=jnp.float32)
    for piece, spot in ((second, slice(0, channels)), (first, slice(channels, None))):
        keep_ref[:, spot] = jnp.where(mine == 0, piece[:half], piece[half:])
        give_ref[:, spot] = jnp.where(mine == 0, piece[half:], piece[:half]).astype(jnp.bfloat16)


def digits(size):
    found = []
    factor = 2
    while size > 1:
        while size % factor == 0:
            found.append(factor)
            size //= factor
        factor += 1
    return found


def plan(n_outer, n_inner):
    steps = []
    stride = 1
    for size in (n_inner, n_outer):
        for radix in digits(size):
            steps.append((stride, radix))
            stride *= radix
    return steps


def linear_index():
    return lax.axis_index("outer") * lax.axis_size("inner") + lax.axis_index("inner")


def shifted(value, count, stride, radix, amount):
    perm = []
    for source in range(count):
        digit = (source // stride) % radix
        target = source + ((digit + amount) % radix - digit) * stride
        perm.append((source, target))
    return lax.ppermute(value, ("outer", "inner"), perm)


def turn(value, count, stride, radix):
    sent = value.astype(jnp.bfloat16)
    mine = (linear_index() // stride) % radix
    parts = jnp.stack([sent] + [shifted(sent, count, stride, radix, k) for k in range(1, radix)])
    total = jnp.zeros(value.shape, jnp.float32)
    for owner in range(radix):
        total = total + parts[(mine - owner) % radix].astype(jnp.float32)
    return total


def swap_stages(steps):
    masks = [stride for stride, radix in steps if radix == 2]
    even = len(masks) // 2 * 2
    return [masks[k : k + 2] for k in range(0, even, 2)], [[mask] for mask in masks[even:]]


def swap_sum(value, count, orders):
    sent = value.astype(jnp.bfloat16)

    def partner(pick):
        masks = []
        for stage in orders:
            mask = 0
            for k in pick:
                mask ^= stage[k]
            masks.append(mask)
        perm = [(source, source ^ masks[source % 2]) for source in range(count)]
        return lax.ppermute(sent, ("outer", "inner"), perm).astype(jnp.float32)

    if len(orders[0]) == 1:
        return sent.astype(jnp.float32) + partner((0,))
    near, far, both = partner((0,)), partner((1,)), partner((0, 1))
    return (sent.astype(jnp.float32) + near) + (far + both)


def pair_perm(count):
    return [(source, source ^ 1) for source in range(count)]


def exchange(keep, give, mine):
    n_outer, n_inner = lax.axis_size("outer"), lax.axis_size("inner")
    count = n_outer * n_inner
    steps = plan(n_outer, n_inner)[1:]
    got = lax.ppermute(give, ("outer", "inner"), pair_perm(count))
    value = keep + got.astype(jnp.float32)
    quads, singles = swap_stages(steps)
    cut = len(quads) // 2
    for even, odd in zip(quads + singles, quads[cut:] + quads[:cut] + singles):
        value = swap_sum(value, count, (even, odd))
    for stride, radix in steps:
        if radix != 2:
            value = turn(value, count, stride, radix)
    value = value.astype(jnp.bfloat16)
    other = lax.ppermute(value, ("outer", "inner"), pair_perm(count))
    return value, other


VMEM = pl.BlockSpec(memory_space=pltpu.VMEM)
HBM = pl.BlockSpec(memory_space=pltpu.HBM)
SMEM = pl.BlockSpec(memory_space=pltpu.SMEM)


def stay(value):
    return pltpu.with_memory_space_constraint(value, pltpu.HBM)


def shards(
    images,
    cotangent,
    conv_weight,
    conv_bias,
    norm_gain,
    norm_bias,
    expand_weight,
    expand_bias,
    reduce_weight,
    layer_scale,
    right_first,
    right_second,
):
    count = lax.axis_size("outer") * lax.axis_size("inner")
    scale = jnp.float32(1.0) / count
    extent, width = images.shape[1], images.shape[3]
    kernel = conv_weight.shape[0]
    hidden_units = expand_weight.shape[1]
    rank = right_first.shape[1]
    rows, half, total = extent * ROW, rank // 2, width + hidden_units
    slabs = width // LANES
    bf16, f32 = jnp.bfloat16, jnp.float32
    mine = (linear_index() % 2).astype(jnp.int32).reshape(1)
    keep, give, normed, activated, grad, hid = pl.pallas_call(
        phase_one,
        out_shape=(
            jax.ShapeDtypeStruct((half, total), f32),
            jax.ShapeDtypeStruct((half, total), bf16),
            jax.ShapeDtypeStruct((rows, width), bf16),
            jax.ShapeDtypeStruct((rows, hidden_units), bf16),
            jax.ShapeDtypeStruct((rows, width), bf16),
            jax.ShapeDtypeStruct((rows, hidden_units), bf16),
        ),
        in_specs=[SMEM] + [HBM] * 12,
        out_specs=(VMEM,) * 6,
        scratch_shapes=[
            pltpu.VMEM(images.shape[1:], bf16),
            pltpu.VMEM(images.shape[1:], bf16),
            pltpu.VMEM(conv_weight.shape, f32),
            pltpu.VMEM((width,), f32),
            pltpu.VMEM((width,), f32),
            pltpu.VMEM((width,), f32),
            pltpu.VMEM((width,), f32),
            pltpu.VMEM((hidden_units,), f32),
            pltpu.VMEM((slabs, extent + kernel - 1, 2 * ROW, LANES), f32),
            pltpu.VMEM((slabs, rows, LANES), f32),
            pltpu.VMEM(expand_weight.shape, bf16),
            pltpu.VMEM(reduce_weight.shape, bf16),
            pltpu.VMEM((rows, hidden_units), f32),
            pltpu.VMEM((rank, hidden_units), f32),
            pltpu.VMEM((rank, width), f32),
            pltpu.VMEM((half, total), f32),
            pltpu.VMEM((half, total), f32),
            pltpu.SemaphoreType.DMA((11,)),
            pltpu.SemaphoreType.DMA((hidden_units // BLOCK,)),
        ],
        compiler_params=pltpu.CompilerParams(vmem_limit_bytes=40 * 1024 * 1024),
        name="phase_one",
    )(
        mine,
        stay(images),
        stay(cotangent),
        stay(conv_weight),
        stay(conv_bias),
        stay(norm_gain),
        stay(norm_bias),
        stay(expand_weight),
        stay(expand_bias),
        stay(reduce_weight),
        stay(layer_scale),
        stay(right_first.T),
        stay(right_second.T),
    )
    value, other = exchange(keep, give, mine)
    keep, give = pl.pallas_call(
        phase_two,
        out_shape=(
            jax.ShapeDtypeStruct((half, total), f32),
            jax.ShapeDtypeStruct((half, total), bf16),
        ),
        in_specs=[SMEM] + [VMEM] * 6,
        out_specs=(VMEM, VMEM),
        compiler_params=pltpu.CompilerParams(vmem_limit_bytes=40 * 1024 * 1024),
        name="phase_two",
    )(mine, value, other, normed, activated, grad, hid)
    value, other = exchange(keep, give, mine)
    low = jnp.where(mine[0] == 0, value, other)
    high = jnp.where(mine[0] == 0, other, value)
    both = jnp.concatenate([low, high], axis=0).astype(f32) * scale
    return (both[:, width:].T, both[:, :width].T)


def solution(mesh):
    in_specs = (
        P(("outer", "inner"), None, None, None),
        P(("outer", "inner"), None, None, None),
        P(),
        P(),
        P(),
        P(),
        P(),
        P(),
        P(),
        P(),
        P(),
        P(),
    )
    out_specs = (P(), P())
    return jax.shard_map(shards, mesh=mesh, in_specs=in_specs, out_specs=out_specs, check_vma=False)
```

```python
import functools

import jax
import jax.numpy as jnp
from jax import lax
from jax.experimental import pallas as pl
from jax.experimental.pallas import tpu as pltpu
from jax.sharding import PartitionSpec as P

LANES = 128
ROW = 16
LEFT = 8
BLOCK = 512
TALL = 7
PIECE = 1024


def phase_one(
    mine_ref,
    images_hbm,
    cotangent_hbm,
    taps_hbm,
    conv_bias_hbm,
    gain_hbm,
    norm_bias_hbm,
    expand_hbm,
    expand_bias_hbm,
    reduce_hbm,
    layer_scale_hbm,
    first_hbm,
    second_hbm,
    keep_ref,
    give_ref,
    normed_ref,
    activated_ref,
    grad_ref,
    hid_ref,
    image,
    cot,
    taps,
    conv_bias,
    gain,
    norm_bias,
    layer_scale,
    expand_bias,
    wide,
    conv,
    expand,
    reduce,
    back,
    first,
    second,
    low,
    high,
    sems,
    block_sems,
):
    extent, channels = images_hbm.shape[1], images_hbm.shape[3]
    kernel = taps_hbm.shape[0]
    margin = kernel // 2
    hidden_units = expand_hbm.shape[1]
    blocks = hidden_units // BLOCK
    slabs = channels // LANES
    half = keep_ref.shape[0]
    rows = extent * ROW
    nt = (((1,), (1,)), ((), ()))

    pairs = [
        (images_hbm.at[0], image),
        (taps_hbm, taps),
        (cotangent_hbm.at[0], cot),
        (layer_scale_hbm, layer_scale),
        (conv_bias_hbm, conv_bias),
        (gain_hbm, gain),
        (norm_bias_hbm, norm_bias),
        (expand_bias_hbm, expand_bias),
        (second_hbm, second),
        (first_hbm, first),
        (expand_hbm, expand),
    ]
    copies = [pltpu.make_async_copy(src, dst, sems.at[k]) for k, (src, dst) in enumerate(pairs)]

    def reduce_copy(j):
        cut = pl.ds(pl.multiple_of(j * BLOCK, BLOCK), BLOCK)
        return pltpu.make_async_copy(reduce_hbm.at[cut, :], reduce.at[cut, :], block_sems.at[j])

    for copy in copies[:5]:
        copy.start()
    for j in range(blocks):
        reduce_copy(j).start()
    for copy in copies[5:]:
        copy.start()

    wide[...] = jnp.zeros(wide.shape, jnp.float32)
    grad_ref[...] = jnp.zeros(grad_ref.shape, jnp.bfloat16)
    copies[0].wait()
    for row in range(extent):
        for slab in range(slabs):
            piece = image[row, :, slab * LANES : (slab + 1) * LANES].astype(jnp.float32)
            wide[slab, margin + row, LEFT : LEFT + extent, :] = piece
    copies[2].wait()
    copies[3].wait()
    for row in range(extent):
        piece = cot[row].astype(jnp.float32) * layer_scale[...].reshape(1, channels)
        grad_ref[row * ROW : row * ROW + extent, :] = piece.astype(jnp.bfloat16)
    copies[1].wait()
    copies[4].wait()

    def conv_tile(slab, top, tall):
        lanes = pl.ds(pl.multiple_of(slab * LANES, LANES), LANES)
        total = jnp.broadcast_to(conv_bias[lanes].reshape(1, 1, LANES), (tall, ROW, LANES))
        for col in range(kernel):
            start = LEFT - margin + col
            seen = wide[slab, pl.ds(top, tall + kernel - 1), start : start + ROW, :]
            for row in range(kernel):
                tap = taps[row, col : col + 1, lanes].reshape(1, 1, LANES)
                total = total + seen[row : row + tall] * tap
        spot = pl.ds(pl.multiple_of(top * ROW, ROW), tall * ROW)
        conv[slab, spot, :] = total.reshape(tall * ROW, LANES)

    tiles = extent // TALL
    per = slabs * tiles // blocks
    assert tiles * TALL == extent and per * blocks == slabs * tiles

    def both_step(j, _):
        reduce_copy(j).wait()
        cut = pl.ds(pl.multiple_of(j * BLOCK, BLOCK), BLOCK)
        back[:, cut] = lax.dot_general(
            grad_ref[...], reduce[cut, :], nt, preferred_element_type=jnp.float32
        )
        for k in range(per):
            step = j * per + k
            conv_tile(step // tiles, (step % tiles) * TALL, TALL)
        return 0

    lax.fori_loop(0, blocks, both_step, 0)

    added = conv[0]
    for slab in range(1, slabs):
        added = added + conv[slab]
    center = jnp.sum(added, axis=-1, keepdims=True) * (1.0 / channels)
    added = jnp.zeros((rows, LANES), jnp.float32)
    for slab in range(slabs):
        away = conv[slab] - center
        added = added + away * away
    spread = jnp.sum(added, axis=-1, keepdims=True) * (1.0 / channels)
    inverse = lax.rsqrt(spread + 1e-06)
    place = lax.broadcasted_iota(jnp.int32, (rows, LANES), 0)
    real = lax.rem(place, ROW) < extent
    for copy in copies[5:]:
        copy.wait()
    for slab in range(slabs):
        lanes = slice(slab * LANES, (slab + 1) * LANES)
        value = (conv[slab] - center) * inverse * gain[lanes].reshape(1, LANES) + norm_bias[lanes].reshape(1, LANES)
        normed_ref[:, lanes] = jnp.where(real, value, 0.0).astype(jnp.bfloat16)

    normed = normed_ref[...]
    thin_second = lax.dot_general(
        second[...].astype(jnp.bfloat16), grad_ref[...], nt, preferred_element_type=jnp.float32
    ).astype(jnp.bfloat16)
    thin = jnp.zeros((first.shape[0], rows), jnp.float32)
    for start in range(0, hidden_units, PIECE):
        cut = slice(start, start + PIECE)
        hidden = jnp.dot(normed, expand[:, cut], preferred_element_type=jnp.float32)
        hidden = hidden + expand_bias[cut].reshape(1, PIECE)
        cdf = 0.5 * (1.0 + lax.erf(hidden * 0.7071067811865476))
        slope = cdf + hidden * jnp.exp(-0.5 * hidden * hidden) * 0.3989422804014327
        activated = (hidden * cdf).astype(jnp.bfloat16)
        hid = (back[:, cut] * slope).astype(jnp.bfloat16)
        activated_ref[:, cut] = activated
        hid_ref[:, cut] = hid
        thin = thin + lax.dot_general(
            first[:, cut].astype(jnp.bfloat16), hid, nt, preferred_element_type=jnp.float32
        )
        sums = jnp.dot(thin_second, activated, preferred_element_type=jnp.float32)
        spot = slice(channels + start, channels + start + PIECE)
        low[:, spot] = sums[:half]
        high[:, spot] = sums[half:]
    sums = jnp.dot(thin.astype(jnp.bfloat16), normed, preferred_element_type=jnp.float32)
    low[:, :channels] = sums[:half]
    high[:, :channels] = sums[half:]
    mine = mine_ref[0]

    @pl.when(mine == 0)
    def _():
        keep_ref[...] = low[...]
        give_ref[...] = high[...].astype(jnp.bfloat16)

    @pl.when(mine != 0)
    def _():
        keep_ref[...] = high[...]
        give_ref[...] = low[...].astype(jnp.bfloat16)


def eliminate(gram_matrix, size):
    wide = 2 * size
    spot = lax.broadcasted_iota(jnp.int32, (size, size), 0)
    across = lax.broadcasted_iota(jnp.int32, (size, size), 1)
    eye = jnp.where(spot == across, 1.0, 0.0).astype(jnp.float32)
    work = jnp.concatenate([gram_matrix, eye], axis=1)
    down = lax.broadcasted_iota(jnp.int32, (size, wide), 0)
    group = 4
    for base in range(0, size, group):
        cols = [
            jnp.broadcast_to(work[:, base + b : base + b + 1], (size, wide)) for b in range(group)
        ]
        rows = [work[base + b : base + b + 1, :] for b in range(group)]
        for b in range(group):
            scale = lax.rsqrt(cols[b][base + b : base + b + 1, :])
            rows[b] = rows[b] * scale
            cols[b] = cols[b] * scale
            for c in range(b + 1, group):
                factor = cols[b][base + c : base + c + 1, :]
                rows[c] = rows[c] - factor * rows[b]
                cols[c] = cols[c] - cols[b] * factor
        change = jnp.zeros((size, wide), jnp.float32)
        for b in range(group):
            change = change + cols[b] * rows[b]
        work = jnp.where(down >= base + group, work - change, work)
        for b in range(group):
            work = jnp.where(down == base + b, rows[b], work)
    return work[:, size:]


def phase_two(
    mine_ref, value_ref, other_ref, normed_ref, activated_ref, grad_ref, hid_ref, keep_ref, give_ref
):
    channels = normed_ref.shape[1]
    half = value_ref.shape[0]
    mine = mine_ref[0]
    value = value_ref[...]
    other = other_ref[...]
    low = jnp.where(mine == 0, value, other)
    high = jnp.where(mine == 0, other, value)
    both = jnp.concatenate([low, high], axis=0)
    nt = (((1,), (1,)), ((), ()))
    bases = []
    for part in (both[:, :channels], both[:, channels:]):
        gram_matrix = lax.dot_general(part, part, nt, preferred_element_type=jnp.float32)
        inverse = eliminate(gram_matrix, 2 * half)
        coarse = inverse.astype(jnp.bfloat16)
        fine = (inverse - coarse.astype(jnp.float32)).astype(jnp.bfloat16)
        basis = jnp.dot(coarse, part, preferred_element_type=jnp.float32)
        basis = basis + jnp.dot(fine, part, preferred_element_type=jnp.float32)
        bases.append(basis.astype(jnp.bfloat16))
    thin = lax.dot_general(bases[0], normed_ref[...], nt, preferred_element_type=jnp.float32)
    first = jnp.dot(thin.astype(jnp.bfloat16), hid_ref[...], preferred_element_type=jnp.float32)
    thin = lax.dot_general(bases[1], activated_ref[...], nt, preferred_element_type=jnp.float32)
    second = jnp.dot(thin.astype(jnp.bfloat16), grad_ref[...], preferred_element_type=jnp.float32)
    for piece, spot in ((second, slice(0, channels)), (first, slice(channels, None))):
        keep_ref[:, spot] = jnp.where(mine == 0, piece[:half], piece[half:])
        give_ref[:, spot] = jnp.where(mine == 0, piece[half:], piece[:half]).astype(jnp.bfloat16)


def phase_three(
    factor, mine_ref, value_ref, other_ref, second_hbm, first_hbm, second, first, sems
):
    half, channels = value_ref.shape[0], second.shape[1]
    mine = mine_ref[0]
    copies = (
        pltpu.make_async_copy(first, first_hbm, sems.at[0]),
        pltpu.make_async_copy(second, second_hbm, sems.at[1]),
    )
    for spot, target, copy in (
        (slice(channels, None), first, copies[0]),
        (slice(0, channels), second, copies[1]),
    ):
        value = value_ref[:, spot].astype(jnp.float32) * factor
        other = other_ref[:, spot].astype(jnp.float32) * factor
        target[:half, :] = jnp.where(mine == 0, value, other)
        target[half:, :] = jnp.where(mine == 0, other, value)
        copy.start()
    for copy in copies:
        copy.wait()


def digits(size):
    found = []
    factor = 2
    while size > 1:
        while size % factor == 0:
            found.append(factor)
            size //= factor
        factor += 1
    return found


def plan(n_outer, n_inner):
    steps = []
    stride = 1
    for size in (n_inner, n_outer):
        for radix in digits(size):
            steps.append((stride, radix))
            stride *= radix
    return steps


def linear_index():
    return lax.axis_index("outer") * lax.axis_size("inner") + lax.axis_index("inner")


def shifted(value, count, stride, radix, amount):
    perm = []
    for source in range(count):
        digit = (source // stride) % radix
        target = source + ((digit + amount) % radix - digit) * stride
        perm.append((source, target))
    return lax.ppermute(value, ("outer", "inner"), perm)


def turn(value, count, stride, radix):
    sent = value.astype(jnp.bfloat16)
    mine = (linear_index() // stride) % radix
    parts = jnp.stack([sent] + [shifted(sent, count, stride, radix, k) for k in range(1, radix)])
    total = jnp.zeros(value.shape, jnp.float32)
    for owner in range(radix):
        total = total + parts[(mine - owner) % radix].astype(jnp.float32)
    return total


def swap_stages(steps):
    masks = [stride for stride, radix in steps if radix == 2]
    even = len(masks) // 2 * 2
    return [masks[k : k + 2] for k in range(0, even, 2)], [[mask] for mask in masks[even:]]


def swap_sum(value, count, orders):
    sent = value.astype(jnp.bfloat16)

    def partner(pick):
        masks = []
        for stage in orders:
            mask = 0
            for k in pick:
                mask ^= stage[k]
            masks.append(mask)
        perm = [(source, source ^ masks[source % 2]) for source in range(count)]
        return lax.ppermute(sent, ("outer", "inner"), perm).astype(jnp.float32)

    if len(orders[0]) == 1:
        return sent.astype(jnp.float32) + partner((0,))
    near, far, both = partner((0,)), partner((1,)), partner((0, 1))
    return (sent.astype(jnp.float32) + near) + (far + both)


def pair_perm(count):
    return [(source, source ^ 1) for source in range(count)]


def exchange(keep, give, mine):
    n_outer, n_inner = lax.axis_size("outer"), lax.axis_size("inner")
    count = n_outer * n_inner
    steps = plan(n_outer, n_inner)[1:]
    got = lax.ppermute(give, ("outer", "inner"), pair_perm(count))
    value = keep + got.astype(jnp.float32)
    quads, singles = swap_stages(steps)
    cut = len(quads) // 2
    for even, odd in zip(quads + singles, quads[cut:] + quads[:cut] + singles):
        value = swap_sum(value, count, (even, odd))
    for stride, radix in steps:
        if radix != 2:
            value = turn(value, count, stride, radix)
    value = value.astype(jnp.bfloat16)
    other = lax.ppermute(value, ("outer", "inner"), pair_perm(count))
    return value, other


VMEM = pl.BlockSpec(memory_space=pltpu.VMEM)
HBM = pl.BlockSpec(memory_space=pltpu.HBM)
SMEM = pl.BlockSpec(memory_space=pltpu.SMEM)


def stay(value):
    return pltpu.with_memory_space_constraint(value, pltpu.HBM)


def shards(
    images,
    cotangent,
    conv_weight,
    conv_bias,
    norm_gain,
    norm_bias,
    expand_weight,
    expand_bias,
    reduce_weight,
    layer_scale,
    right_first,
    right_second,
):
    count = lax.axis_size("outer") * lax.axis_size("inner")
    scale = 1.0 / count
    extent, width = images.shape[1], images.shape[3]
    kernel = conv_weight.shape[0]
    hidden_units = expand_weight.shape[1]
    rank = right_first.shape[1]
    rows, half, total = extent * ROW, rank // 2, width + hidden_units
    slabs = width // LANES
    bf16, f32 = jnp.bfloat16, jnp.float32
    mine = (linear_index() % 2).astype(jnp.int32).reshape(1)
    keep, give, normed, activated, grad, hid = pl.pallas_call(
        phase_one,
        out_shape=(
            jax.ShapeDtypeStruct((half, total), f32),
            jax.ShapeDtypeStruct((half, total), bf16),
            jax.ShapeDtypeStruct((rows, width), bf16),
            jax.ShapeDtypeStruct((rows, hidden_units), bf16),
            jax.ShapeDtypeStruct((rows, width), bf16),
            jax.ShapeDtypeStruct((rows, hidden_units), bf16),
        ),
        in_specs=[SMEM] + [HBM] * 12,
        out_specs=(VMEM,) * 6,
        scratch_shapes=[
            pltpu.VMEM(images.shape[1:], bf16),
            pltpu.VMEM(images.shape[1:], bf16),
            pltpu.VMEM(conv_weight.shape, f32),
            pltpu.VMEM((width,), f32),
            pltpu.VMEM((width,), f32),
            pltpu.VMEM((width,), f32),
            pltpu.VMEM((width,), f32),
            pltpu.VMEM((hidden_units,), f32),
            pltpu.VMEM((slabs, extent + kernel - 1, 2 * ROW, LANES), f32),
            pltpu.VMEM((slabs, rows, LANES), f32),
            pltpu.VMEM(expand_weight.shape, bf16),
            pltpu.VMEM(reduce_weight.shape, bf16),
            pltpu.VMEM((rows, hidden_units), f32),
            pltpu.VMEM((rank, hidden_units), f32),
            pltpu.VMEM((rank, width), f32),
            pltpu.VMEM((half, total), f32),
            pltpu.VMEM((half, total), f32),
            pltpu.SemaphoreType.DMA((11,)),
            pltpu.SemaphoreType.DMA((hidden_units // BLOCK,)),
        ],
        compiler_params=pltpu.CompilerParams(vmem_limit_bytes=40 * 1024 * 1024),
        name="phase_one",
    )(
        mine,
        stay(images),
        stay(cotangent),
        stay(conv_weight),
        stay(conv_bias),
        stay(norm_gain),
        stay(norm_bias),
        stay(expand_weight),
        stay(expand_bias),
        stay(reduce_weight),
        stay(layer_scale),
        stay(right_first.T),
        stay(right_second.T),
    )
    value, other = exchange(keep, give, mine)
    keep, give = pl.pallas_call(
        phase_two,
        out_shape=(
            jax.ShapeDtypeStruct((half, total), f32),
            jax.ShapeDtypeStruct((half, total), bf16),
        ),
        in_specs=[SMEM] + [VMEM] * 6,
        out_specs=(VMEM, VMEM),
        compiler_params=pltpu.CompilerParams(vmem_limit_bytes=40 * 1024 * 1024),
        name="phase_two",
    )(mine, value, other, normed, activated, grad, hid)
    value, other = exchange(keep, give, mine)
    second, first = pl.pallas_call(
        functools.partial(phase_three, scale),
        out_shape=(
            jax.ShapeDtypeStruct((rank, width), f32),
            jax.ShapeDtypeStruct((rank, hidden_units), f32),
        ),
        in_specs=[SMEM, VMEM, VMEM],
        out_specs=(HBM, HBM),
        scratch_shapes=[
            pltpu.VMEM((rank, width), f32),
            pltpu.VMEM((rank, hidden_units), f32),
            pltpu.SemaphoreType.DMA((2,)),
        ],
        compiler_params=pltpu.CompilerParams(vmem_limit_bytes=8 * 1024 * 1024),
        name="phase_three",
    )(mine, value, other)
    return (first.T, second.T)


def solution(mesh):
    in_specs = (
        P(("outer", "inner"), None, None, None),
        P(("outer", "inner"), None, None, None),
        P(),
        P(),
        P(),
        P(),
        P(),
        P(),
        P(),
        P(),
        P(),
        P(),
    )
    out_specs = (P(), P())
    return jax.shard_map(shards, mesh=mesh, in_specs=in_specs, out_specs=out_specs, check_vma=False)
```

```python
import functools

import jax
import jax.numpy as jnp
from jax import lax
from jax.experimental import pallas as pl
from jax.experimental.pallas import tpu as pltpu
from jax.sharding import PartitionSpec as P

LANES = 128
ROW = 16
LEFT = 8
BLOCK = 512
TALL = 7
SUBLANES = 8
GROUP = 8
PIECE = 512


def phase_one(
    mine_ref,
    images_hbm,
    cotangent_hbm,
    taps_hbm,
    conv_bias_hbm,
    gain_hbm,
    norm_bias_hbm,
    expand_hbm,
    expand_bias_hbm,
    reduce_hbm,
    layer_scale_hbm,
    first_hbm,
    second_hbm,
    keep_ref,
    give_ref,
    normed_ref,
    activated_ref,
    grad_ref,
    hid_ref,
    image,
    cot,
    taps,
    conv_bias,
    gain,
    norm_bias,
    layer_scale,
    expand_bias,
    wide,
    conv,
    expand,
    reduce,
    back,
    first,
    second,
    low,
    high,
    sems,
    block_sems,
):
    extent, channels = images_hbm.shape[1], images_hbm.shape[3]
    kernel = taps_hbm.shape[0]
    margin = kernel // 2
    hidden_units = expand_hbm.shape[1]
    blocks = hidden_units // BLOCK
    slabs = channels // LANES
    half = keep_ref.shape[0]
    rows = extent * ROW
    nt = (((1,), (1,)), ((), ()))

    pairs = [
        (images_hbm.at[0], image),
        (taps_hbm, taps),
        (cotangent_hbm.at[0], cot),
        (layer_scale_hbm, layer_scale),
        (conv_bias_hbm, conv_bias),
        (gain_hbm, gain),
        (norm_bias_hbm, norm_bias),
        (expand_bias_hbm, expand_bias),
        (second_hbm, second),
        (first_hbm, first),
        (expand_hbm, expand),
    ]
    copies = [pltpu.make_async_copy(src, dst, sems.at[k]) for k, (src, dst) in enumerate(pairs)]

    def reduce_copy(j):
        cut = pl.ds(pl.multiple_of(j * BLOCK, BLOCK), BLOCK)
        return pltpu.make_async_copy(reduce_hbm.at[cut, :], reduce.at[cut, :], block_sems.at[j])

    for copy in copies[:5]:
        copy.start()
    for j in range(blocks):
        reduce_copy(j).start()
    for copy in copies[5:]:
        copy.start()

    wide[...] = jnp.zeros(wide.shape, jnp.float32)
    grad_ref[...] = jnp.zeros(grad_ref.shape, jnp.bfloat16)
    copies[0].wait()
    for row in range(extent):
        for slab in range(slabs):
            piece = image[row, :, slab * LANES : (slab + 1) * LANES].astype(jnp.float32)
            wide[slab, margin + row, LEFT : LEFT + extent, :] = piece
    copies[2].wait()
    copies[3].wait()
    for row in range(extent):
        piece = cot[row].astype(jnp.float32) * layer_scale[...].reshape(1, channels)
        grad_ref[row * ROW : row * ROW + extent, :] = piece.astype(jnp.bfloat16)
    copies[1].wait()
    copies[4].wait()

    def conv_tile(slab, top, tall):
        lanes = pl.ds(pl.multiple_of(slab * LANES, LANES), LANES)
        total = jnp.broadcast_to(conv_bias[lanes].reshape(1, 1, LANES), (tall, ROW, LANES))
        for col in range(kernel):
            start = LEFT - margin + col
            seen = wide[slab, pl.ds(top, tall + kernel - 1), start : start + ROW, :]
            for row in range(kernel):
                tap = taps[row, col : col + 1, lanes].reshape(1, 1, LANES)
                total = total + seen[row : row + tall] * tap
        spot = pl.ds(pl.multiple_of(top * ROW, ROW), tall * ROW)
        conv[slab, spot, :] = total.reshape(tall * ROW, LANES)

    tiles = extent // TALL
    per = slabs * tiles // blocks
    assert tiles * TALL == extent and per * blocks == slabs * tiles

    def both_step(j, _):
        reduce_copy(j).wait()
        cut = pl.ds(pl.multiple_of(j * BLOCK, BLOCK), BLOCK)
        back[:, cut] = lax.dot_general(
            grad_ref[...], reduce[cut, :], nt, preferred_element_type=jnp.float32
        )
        for k in range(per):
            step = j * per + k
            conv_tile(step // tiles, (step % tiles) * TALL, TALL)
        return 0

    lax.fori_loop(0, blocks, both_step, 0)

    for copy in copies[5:]:
        copy.wait()
    thin_second = lax.dot_general(
        second[...].astype(jnp.bfloat16), grad_ref[...], nt, preferred_element_type=jnp.float32
    ).astype(jnp.bfloat16)
    added = conv[0]
    for slab in range(1, slabs):
        added = added + conv[slab]
    center = jnp.sum(added, axis=-1, keepdims=True) * (1.0 / channels)
    added = jnp.zeros((rows, LANES), jnp.float32)
    for slab in range(slabs):
        away = conv[slab] - center
        added = added + away * away
    spread = jnp.sum(added, axis=-1, keepdims=True) * (1.0 / channels)
    inverse = lax.rsqrt(spread + 1e-06)
    place = lax.broadcasted_iota(jnp.int32, (rows, LANES), 0)
    real = lax.rem(place, ROW) < extent
    for slab in range(slabs):
        lanes = slice(slab * LANES, (slab + 1) * LANES)
        value = (conv[slab] - center) * inverse * gain[lanes].reshape(1, LANES) + norm_bias[lanes].reshape(1, LANES)
        normed_ref[:, lanes] = jnp.where(real, value, 0.0).astype(jnp.bfloat16)

    normed = normed_ref[...]
    thin = jnp.zeros((first.shape[0], rows), jnp.float32)

    def expanded(start):
        cut = slice(start, start + PIECE)
        hidden = jnp.dot(normed, expand[:, cut], preferred_element_type=jnp.float32)
        return hidden + expand_bias[cut].reshape(1, PIECE)

    starts = range(0, hidden_units, PIECE)
    ahead = expanded(0)
    for start in starts:
        cut = slice(start, start + PIECE)
        hidden = ahead
        if start + PIECE < hidden_units:
            ahead = expanded(start + PIECE)
        cdf = 1.0 + lax.erf(hidden * 0.7071067811865476)
        bell = lax.exp2(hidden * hidden * -0.7213475204444817)
        slope = cdf + (hidden * 0.7978845608028654) * bell
        activated = (hidden * cdf).astype(jnp.bfloat16)
        hid = (back[:, cut] * slope).astype(jnp.bfloat16)
        activated_ref[:, cut] = activated
        hid_ref[:, cut] = hid
        thin = thin + lax.dot_general(
            first[:, cut].astype(jnp.bfloat16), hid, nt, preferred_element_type=jnp.float32
        )
        sums = jnp.dot(thin_second, activated, preferred_element_type=jnp.float32)
        spot = slice(channels + start, channels + start + PIECE)
        low[:, spot] = sums[:half]
        high[:, spot] = sums[half:]
    sums = jnp.dot(thin.astype(jnp.bfloat16), normed, preferred_element_type=jnp.float32)
    low[:, :channels] = sums[:half]
    high[:, :channels] = sums[half:]
    mine = mine_ref[0]

    @pl.when(mine == 0)
    def _():
        keep_ref[...] = low[...]
        give_ref[...] = high[...].astype(jnp.bfloat16)

    @pl.when(mine != 0)
    def _():
        keep_ref[...] = high[...]
        give_ref[...] = low[...].astype(jnp.bfloat16)


def eliminate(gram_matrix, size):
    wide = 2 * size
    spot = lax.broadcasted_iota(jnp.int32, (size, size), 0)
    across = lax.broadcasted_iota(jnp.int32, (size, size), 1)
    eye = jnp.where(spot == across, 1.0, 0.0).astype(jnp.float32)
    work = jnp.concatenate([gram_matrix, eye], axis=1)
    down = lax.broadcasted_iota(jnp.int32, (SUBLANES, wide), 0)
    tiles = [work[k : k + SUBLANES, :] for k in range(0, size, SUBLANES)]
    for base in range(0, size, GROUP):
        top, spot = base // SUBLANES, base % SUBLANES
        count = len(tiles) - top
        cols = [
            [
                jnp.broadcast_to(tile[:, base + b : base + b + 1], (SUBLANES, wide))
                for tile in tiles[top:]
            ]
            for b in range(GROUP)
        ]
        rows = [tiles[top][spot + b : spot + b + 1, :] for b in range(GROUP)]
        for b in range(GROUP):
            scale = lax.rsqrt(cols[b][0][spot + b : spot + b + 1, :])
            rows[b] = rows[b] * scale
            cols[b] = [col * scale for col in cols[b]]
            for c in range(b + 1, GROUP):
                factor = cols[b][0][spot + c : spot + c + 1, :]
                rows[c] = rows[c] - factor * rows[b]
                cols[c] = [cols[c][k] - cols[b][k] * factor for k in range(count)]
        for k in range(count):
            change = cols[0][k] * rows[0]
            for b in range(1, GROUP):
                change = change + cols[b][k] * rows[b]
            tile = tiles[top + k]
            if k:
                tile = tile - change
            else:
                if spot + GROUP < SUBLANES:
                    tile = jnp.where(down >= spot + GROUP, tile - change, tile)
                for b in range(GROUP):
                    tile = jnp.where(down == spot + b, rows[b], tile)
            tiles[top + k] = tile
    return jnp.concatenate(tiles, axis=0)[:, size:]


def phase_two(
    mine_ref, value_ref, other_ref, normed_ref, activated_ref, grad_ref, hid_ref, keep_ref, give_ref
):
    channels = normed_ref.shape[1]
    half = value_ref.shape[0]
    mine = mine_ref[0]
    value = value_ref[...]
    other = other_ref[...]
    low = jnp.where(mine == 0, value, other)
    high = jnp.where(mine == 0, other, value)
    both = jnp.concatenate([low, high], axis=0)
    nt = (((1,), (1,)), ((), ()))
    bases = []
    for part in (both[:, :channels], both[:, channels:]):
        gram_matrix = lax.dot_general(part, part, nt, preferred_element_type=jnp.float32)
        inverse = eliminate(gram_matrix, 2 * half)
        coarse = inverse.astype(jnp.bfloat16)
        fine = (inverse - coarse.astype(jnp.float32)).astype(jnp.bfloat16)
        basis = jnp.dot(coarse, part, preferred_element_type=jnp.float32)
        basis = basis + jnp.dot(fine, part, preferred_element_type=jnp.float32)
        bases.append(basis.astype(jnp.bfloat16))
    thin = lax.dot_general(bases[0], normed_ref[...], nt, preferred_element_type=jnp.float32)
    first = jnp.dot(thin.astype(jnp.bfloat16), hid_ref[...], preferred_element_type=jnp.float32)
    thin = lax.dot_general(bases[1], activated_ref[...], nt, preferred_element_type=jnp.float32)
    second = jnp.dot(thin.astype(jnp.bfloat16), grad_ref[...], preferred_element_type=jnp.float32)
    for piece, spot in ((second, slice(0, channels)), (first, slice(channels, None))):
        keep_ref[:, spot] = jnp.where(mine == 0, piece[:half], piece[half:])
        give_ref[:, spot] = jnp.where(mine == 0, piece[half:], piece[:half]).astype(jnp.bfloat16)


def phase_three(
    factor, mine_ref, value_ref, other_ref, second_hbm, first_hbm, second, first, sems
):
    half, channels = value_ref.shape[0], second.shape[1]
    mine = mine_ref[0]
    copies = (
        pltpu.make_async_copy(first, first_hbm, sems.at[0]),
        pltpu.make_async_copy(second, second_hbm, sems.at[1]),
    )
    for spot, target, copy in (
        (slice(channels, None), first, copies[0]),
        (slice(0, channels), second, copies[1]),
    ):
        value = value_ref[:, spot].astype(jnp.float32) * factor
        other = other_ref[:, spot].astype(jnp.float32) * factor
        target[:half, :] = jnp.where(mine == 0, value, other)
        target[half:, :] = jnp.where(mine == 0, other, value)
        copy.start()
    for copy in copies:
        copy.wait()


def digits(size):
    found = []
    factor = 2
    while size > 1:
        while size % factor == 0:
            found.append(factor)
            size //= factor
        factor += 1
    return found


def plan(n_outer, n_inner):
    steps = []
    stride = 1
    for size in (n_inner, n_outer):
        for radix in digits(size):
            steps.append((stride, radix))
            stride *= radix
    return steps


def linear_index():
    return lax.axis_index("outer") * lax.axis_size("inner") + lax.axis_index("inner")


def shifted(value, count, stride, radix, amount):
    perm = []
    for source in range(count):
        digit = (source // stride) % radix
        target = source + ((digit + amount) % radix - digit) * stride
        perm.append((source, target))
    return lax.ppermute(value, ("outer", "inner"), perm)


def turn(value, count, stride, radix):
    sent = value.astype(jnp.bfloat16)
    mine = (linear_index() // stride) % radix
    parts = jnp.stack([sent] + [shifted(sent, count, stride, radix, k) for k in range(1, radix)])
    total = jnp.zeros(value.shape, jnp.float32)
    for owner in range(radix):
        total = total + parts[(mine - owner) % radix].astype(jnp.float32)
    return total


def swap_stages(steps):
    masks = [stride for stride, radix in steps if radix == 2]
    even = len(masks) // 2 * 2
    return [masks[k : k + 2] for k in range(0, even, 2)], [[mask] for mask in masks[even:]]


def swap_sum(value, count, orders):
    sent = value.astype(jnp.bfloat16)

    def partner(pick):
        masks = []
        for stage in orders:
            mask = 0
            for k in pick:
                mask ^= stage[k]
            masks.append(mask)
        perm = [(source, source ^ masks[source % 2]) for source in range(count)]
        return lax.ppermute(sent, ("outer", "inner"), perm).astype(jnp.float32)

    if len(orders[0]) == 1:
        return sent.astype(jnp.float32) + partner((0,))
    near, far, both = partner((0,)), partner((1,)), partner((0, 1))
    return (sent.astype(jnp.float32) + near) + (far + both)


def pair_perm(count):
    return [(source, source ^ 1) for source in range(count)]


def exchange(keep, give, mine):
    n_outer, n_inner = lax.axis_size("outer"), lax.axis_size("inner")
    count = n_outer * n_inner
    steps = plan(n_outer, n_inner)[1:]
    got = lax.ppermute(give, ("outer", "inner"), pair_perm(count))
    value = keep + got.astype(jnp.float32)
    quads, singles = swap_stages(steps)
    cut = len(quads) // 2
    for even, odd in zip(quads + singles, quads[cut:] + quads[:cut] + singles):
        value = swap_sum(value, count, (even, odd))
    for stride, radix in steps:
        if radix != 2:
            value = turn(value, count, stride, radix)
    value = value.astype(jnp.bfloat16)
    other = lax.ppermute(value, ("outer", "inner"), pair_perm(count))
    return value, other


VMEM = pl.BlockSpec(memory_space=pltpu.VMEM)
HBM = pl.BlockSpec(memory_space=pltpu.HBM)
SMEM = pl.BlockSpec(memory_space=pltpu.SMEM)


def stay(value):
    return pltpu.with_memory_space_constraint(value, pltpu.HBM)


def shards(
    images,
    cotangent,
    conv_weight,
    conv_bias,
    norm_gain,
    norm_bias,
    expand_weight,
    expand_bias,
    reduce_weight,
    layer_scale,
    right_first,
    right_second,
):
    count = lax.axis_size("outer") * lax.axis_size("inner")
    scale = 1.0 / count
    extent, width = images.shape[1], images.shape[3]
    kernel = conv_weight.shape[0]
    hidden_units = expand_weight.shape[1]
    rank = right_first.shape[1]
    rows, half, total = extent * ROW, rank // 2, width + hidden_units
    slabs = width // LANES
    bf16, f32 = jnp.bfloat16, jnp.float32
    mine = (linear_index() % 2).astype(jnp.int32).reshape(1)
    keep, give, normed, activated, grad, hid = pl.pallas_call(
        phase_one,
        out_shape=(
            jax.ShapeDtypeStruct((half, total), f32),
            jax.ShapeDtypeStruct((half, total), bf16),
            jax.ShapeDtypeStruct((rows, width), bf16),
            jax.ShapeDtypeStruct((rows, hidden_units), bf16),
            jax.ShapeDtypeStruct((rows, width), bf16),
            jax.ShapeDtypeStruct((rows, hidden_units), bf16),
        ),
        in_specs=[SMEM] + [HBM] * 12,
        out_specs=(VMEM,) * 6,
        scratch_shapes=[
            pltpu.VMEM(images.shape[1:], bf16),
            pltpu.VMEM(images.shape[1:], bf16),
            pltpu.VMEM(conv_weight.shape, f32),
            pltpu.VMEM((width,), f32),
            pltpu.VMEM((width,), f32),
            pltpu.VMEM((width,), f32),
            pltpu.VMEM((width,), f32),
            pltpu.VMEM((hidden_units,), f32),
            pltpu.VMEM((slabs, extent + kernel - 1, 2 * ROW, LANES), f32),
            pltpu.VMEM((slabs, rows, LANES), f32),
            pltpu.VMEM(expand_weight.shape, bf16),
            pltpu.VMEM(reduce_weight.shape, bf16),
            pltpu.VMEM((rows, hidden_units), f32),
            pltpu.VMEM((rank, hidden_units), f32),
            pltpu.VMEM((rank, width), f32),
            pltpu.VMEM((half, total), f32),
            pltpu.VMEM((half, total), f32),
            pltpu.SemaphoreType.DMA((11,)),
            pltpu.SemaphoreType.DMA((hidden_units // BLOCK,)),
        ],
        compiler_params=pltpu.CompilerParams(vmem_limit_bytes=40 * 1024 * 1024),
        name="phase_one",
    )(
        mine,
        stay(images),
        stay(cotangent),
        stay(conv_weight),
        stay(conv_bias),
        stay(norm_gain),
        stay(norm_bias),
        stay(expand_weight),
        stay(expand_bias),
        stay(reduce_weight),
        stay(layer_scale),
        stay(right_first.T),
        stay(right_second.T),
    )
    value, other = exchange(keep, give, mine)
    keep, give = pl.pallas_call(
        phase_two,
        out_shape=(
            jax.ShapeDtypeStruct((half, total), f32),
            jax.ShapeDtypeStruct((half, total), bf16),
        ),
        in_specs=[SMEM] + [VMEM] * 6,
        out_specs=(VMEM, VMEM),
        compiler_params=pltpu.CompilerParams(vmem_limit_bytes=40 * 1024 * 1024),
        name="phase_two",
    )(mine, value, other, normed, activated, grad, hid)
    value, other = exchange(keep, give, mine)
    second, first = pl.pallas_call(
        functools.partial(phase_three, 0.5 * scale),
        out_shape=(
            jax.ShapeDtypeStruct((rank, width), f32),
            jax.ShapeDtypeStruct((rank, hidden_units), f32),
        ),
        in_specs=[SMEM, VMEM, VMEM],
        out_specs=(HBM, HBM),
        scratch_shapes=[
            pltpu.VMEM((rank, width), f32),
            pltpu.VMEM((rank, hidden_units), f32),
            pltpu.SemaphoreType.DMA((2,)),
        ],
        compiler_params=pltpu.CompilerParams(vmem_limit_bytes=8 * 1024 * 1024),
        name="phase_three",
    )(mine, value, other)
    return (first.T, second.T)


def solution(mesh):
    in_specs = (
        P(("outer", "inner"), None, None, None),
        P(("outer", "inner"), None, None, None),
        P(),
        P(),
        P(),
        P(),
        P(),
        P(),
        P(),
        P(),
        P(),
        P(),
    )
    out_specs = (P(), P())
    return jax.shard_map(shards, mesh=mesh, in_specs=in_specs, out_specs=out_specs, check_vma=False)
```

```python
import functools

import jax
import jax.numpy as jnp
from jax import lax
from jax.experimental import pallas as pl
from jax.experimental.pallas import tpu as pltpu
from jax.sharding import PartitionSpec as P

LANES = 128
ROW = 16
LEFT = 8
BLOCK = 512
TALL = 7
SUBLANES = 8
GROUP = 8
PIECE = 512


def phase_one(
    images_hbm,
    cotangent_hbm,
    taps_hbm,
    conv_bias_hbm,
    gain_hbm,
    norm_bias_hbm,
    expand_hbm,
    expand_bias_hbm,
    reduce_hbm,
    layer_scale_hbm,
    first_hbm,
    second_hbm,
    keep_ref,
    give_ref,
    normed_ref,
    activated_ref,
    grad_ref,
    hid_ref,
    image,
    cot,
    taps,
    conv_bias,
    gain,
    norm_bias,
    layer_scale,
    expand_bias,
    wide,
    conv,
    expand,
    reduce,
    back,
    first,
    second,
    low,
    high,
    sems,
    block_sems,
):
    extent, channels = images_hbm.shape[1], images_hbm.shape[3]
    kernel = taps_hbm.shape[0]
    margin = kernel // 2
    hidden_units = expand_hbm.shape[1]
    blocks = hidden_units // BLOCK
    slabs = channels // LANES
    half = keep_ref.shape[0]
    rows = extent * ROW
    nt = (((1,), (1,)), ((), ()))

    pairs = [
        (images_hbm.at[0], image),
        (taps_hbm, taps),
        (cotangent_hbm.at[0], cot),
        (layer_scale_hbm, layer_scale),
        (conv_bias_hbm, conv_bias),
        (gain_hbm, gain),
        (norm_bias_hbm, norm_bias),
        (expand_bias_hbm, expand_bias),
        (second_hbm, second),
        (first_hbm, first),
        (expand_hbm, expand),
    ]
    copies = [pltpu.make_async_copy(src, dst, sems.at[k]) for k, (src, dst) in enumerate(pairs)]

    def reduce_copy(j):
        cut = pl.ds(pl.multiple_of(j * BLOCK, BLOCK), BLOCK)
        return pltpu.make_async_copy(reduce_hbm.at[cut, :], reduce.at[cut, :], block_sems.at[j])

    for copy in copies[:5]:
        copy.start()
    for j in range(blocks):
        reduce_copy(j).start()
    for copy in copies[5:]:
        copy.start()

    wide[...] = jnp.zeros(wide.shape, jnp.float32)
    grad_ref[...] = jnp.zeros(grad_ref.shape, jnp.bfloat16)
    copies[0].wait()
    for row in range(extent):
        for slab in range(slabs):
            piece = image[row, :, slab * LANES : (slab + 1) * LANES].astype(jnp.float32)
            wide[slab, margin + row, LEFT : LEFT + extent, :] = piece
    copies[2].wait()
    copies[3].wait()
    for row in range(extent):
        piece = cot[row].astype(jnp.float32) * layer_scale[...].reshape(1, channels)
        grad_ref[row * ROW : row * ROW + extent, :] = piece.astype(jnp.bfloat16)
    copies[1].wait()
    copies[4].wait()

    def conv_tile(slab, top, tall):
        lanes = pl.ds(pl.multiple_of(slab * LANES, LANES), LANES)
        total = jnp.broadcast_to(conv_bias[lanes].reshape(1, 1, LANES), (tall, ROW, LANES))
        for col in range(kernel):
            start = LEFT - margin + col
            seen = wide[slab, pl.ds(top, tall + kernel - 1), start : start + ROW, :]
            for row in range(kernel):
                tap = taps[row, col : col + 1, lanes].reshape(1, 1, LANES)
                total = total + seen[row : row + tall] * tap
        spot = pl.ds(pl.multiple_of(top * ROW, ROW), tall * ROW)
        conv[slab, spot, :] = total.reshape(tall * ROW, LANES)

    tiles = extent // TALL
    per = slabs * tiles // blocks
    assert tiles * TALL == extent and per * blocks == slabs * tiles

    def both_step(j, _):
        reduce_copy(j).wait()
        cut = pl.ds(pl.multiple_of(j * BLOCK, BLOCK), BLOCK)
        back[:, cut] = lax.dot_general(
            grad_ref[...], reduce[cut, :], nt, preferred_element_type=jnp.float32
        )
        for k in range(per):
            step = j * per + k
            conv_tile(step // tiles, (step % tiles) * TALL, TALL)
        return 0

    lax.fori_loop(0, blocks, both_step, 0)

    for copy in copies[5:]:
        copy.wait()
    thin_second = lax.dot_general(
        second[...].astype(jnp.bfloat16), grad_ref[...], nt, preferred_element_type=jnp.float32
    ).astype(jnp.bfloat16)
    added = conv[0]
    for slab in range(1, slabs):
        added = added + conv[slab]
    center = jnp.sum(added, axis=-1, keepdims=True) * (1.0 / channels)
    added = jnp.zeros((rows, LANES), jnp.float32)
    for slab in range(slabs):
        away = conv[slab] - center
        added = added + away * away
    spread = jnp.sum(added, axis=-1, keepdims=True) * (1.0 / channels)
    inverse = lax.rsqrt(spread + 1e-06)
    place = lax.broadcasted_iota(jnp.int32, (rows, LANES), 0)
    real = lax.rem(place, ROW) < extent
    for slab in range(slabs):
        lanes = slice(slab * LANES, (slab + 1) * LANES)
        value = (conv[slab] - center) * inverse * gain[lanes].reshape(1, LANES) + norm_bias[lanes].reshape(1, LANES)
        normed_ref[:, lanes] = jnp.where(real, value, 0.0).astype(jnp.bfloat16)

    normed = normed_ref[...]
    thin = jnp.zeros((first.shape[0], rows), jnp.float32)

    def expanded(start):
        cut = slice(start, start + PIECE)
        hidden = jnp.dot(normed, expand[:, cut], preferred_element_type=jnp.float32)
        return hidden + expand_bias[cut].reshape(1, PIECE)

    starts = range(0, hidden_units, PIECE)
    ahead = expanded(0)
    for start in starts:
        cut = slice(start, start + PIECE)
        hidden = ahead
        if start + PIECE < hidden_units:
            ahead = expanded(start + PIECE)
        cdf = 1.0 + lax.erf(hidden * 0.7071067811865476)
        bell = lax.exp2(hidden * hidden * -0.7213475204444817)
        slope = cdf + (hidden * 0.7978845608028654) * bell
        activated = (hidden * cdf).astype(jnp.bfloat16)
        hid = (back[:, cut] * slope).astype(jnp.bfloat16)
        activated_ref[:, cut] = activated
        hid_ref[:, cut] = hid
        thin = thin + lax.dot_general(
            first[:, cut].astype(jnp.bfloat16), hid, nt, preferred_element_type=jnp.float32
        )
        sums = jnp.dot(thin_second, activated, preferred_element_type=jnp.float32)
        spot = slice(channels + start, channels + start + PIECE)
        low[:, spot] = sums[:half]
        high[:, spot] = sums[half:]
    sums = jnp.dot(thin.astype(jnp.bfloat16), normed, preferred_element_type=jnp.float32)
    low[:, :channels] = sums[:half]
    high[:, :channels] = sums[half:]
    mine = lax.rem(linear_index(), 2)

    @pl.when(mine == 0)
    def _():
        keep_ref[...] = low[...]
        give_ref[...] = high[...].astype(jnp.bfloat16)

    @pl.when(mine != 0)
    def _():
        keep_ref[...] = high[...]
        give_ref[...] = low[...].astype(jnp.bfloat16)


def eliminate(gram_matrix, size):
    wide = 2 * size
    spot = lax.broadcasted_iota(jnp.int32, (size, size), 0)
    across = lax.broadcasted_iota(jnp.int32, (size, size), 1)
    eye = jnp.where(spot == across, 1.0, 0.0).astype(jnp.float32)
    work = jnp.concatenate([gram_matrix, eye], axis=1)
    down = lax.broadcasted_iota(jnp.int32, (SUBLANES, wide), 0)
    tiles = [work[k : k + SUBLANES, :] for k in range(0, size, SUBLANES)]
    for base in range(0, size, GROUP):
        top, spot = base // SUBLANES, base % SUBLANES
        count = len(tiles) - top
        cols = [
            [
                jnp.broadcast_to(tile[:, base + b : base + b + 1], (SUBLANES, wide))
                for tile in tiles[top:]
            ]
            for b in range(GROUP)
        ]
        rows = [tiles[top][spot + b : spot + b + 1, :] for b in range(GROUP)]
        for b in range(GROUP):
            scale = lax.rsqrt(cols[b][0][spot + b : spot + b + 1, :])
            rows[b] = rows[b] * scale
            cols[b] = [col * scale for col in cols[b]]
            for c in range(b + 1, GROUP):
                factor = cols[b][0][spot + c : spot + c + 1, :]
                rows[c] = rows[c] - factor * rows[b]
                cols[c] = [cols[c][k] - cols[b][k] * factor for k in range(count)]
        for k in range(count):
            change = cols[0][k] * rows[0]
            for b in range(1, GROUP):
                change = change + cols[b][k] * rows[b]
            tile = tiles[top + k]
            if k:
                tile = tile - change
            else:
                if spot + GROUP < SUBLANES:
                    tile = jnp.where(down >= spot + GROUP, tile - change, tile)
                for b in range(GROUP):
                    tile = jnp.where(down == spot + b, rows[b], tile)
            tiles[top + k] = tile
    return jnp.concatenate(tiles, axis=0)[:, size:]


def phase_two(
    value_ref, other_ref, normed_ref, activated_ref, grad_ref, hid_ref, keep_ref, give_ref
):
    channels = normed_ref.shape[1]
    half = value_ref.shape[0]
    mine = lax.rem(linear_index(), 2)
    value = value_ref[...]
    other = other_ref[...]
    low = jnp.where(mine == 0, value, other)
    high = jnp.where(mine == 0, other, value)
    both = jnp.concatenate([low, high], axis=0)
    nt = (((1,), (1,)), ((), ()))
    bases = []
    for part in (both[:, :channels], both[:, channels:]):
        gram_matrix = lax.dot_general(part, part, nt, preferred_element_type=jnp.float32)
        inverse = eliminate(gram_matrix, 2 * half)
        coarse = inverse.astype(jnp.bfloat16)
        fine = (inverse - coarse.astype(jnp.float32)).astype(jnp.bfloat16)
        basis = jnp.dot(coarse, part, preferred_element_type=jnp.float32)
        basis = basis + jnp.dot(fine, part, preferred_element_type=jnp.float32)
        bases.append(basis.astype(jnp.bfloat16))
    thin = lax.dot_general(bases[0], normed_ref[...], nt, preferred_element_type=jnp.float32)
    first = jnp.dot(thin.astype(jnp.bfloat16), hid_ref[...], preferred_element_type=jnp.float32)
    thin = lax.dot_general(bases[1], activated_ref[...], nt, preferred_element_type=jnp.float32)
    second = jnp.dot(thin.astype(jnp.bfloat16), grad_ref[...], preferred_element_type=jnp.float32)
    for piece, spot in ((second, slice(0, channels)), (first, slice(channels, None))):
        keep_ref[:, spot] = jnp.where(mine == 0, piece[:half], piece[half:])
        give_ref[:, spot] = jnp.where(mine == 0, piece[half:], piece[:half]).astype(jnp.bfloat16)


def phase_three(
    factor, value_ref, other_ref, second_hbm, first_hbm, second, first, sems
):
    half, channels = value_ref.shape[0], second.shape[1]
    mine = lax.rem(linear_index(), 2)
    copies = (
        pltpu.make_async_copy(first, first_hbm, sems.at[0]),
        pltpu.make_async_copy(second, second_hbm, sems.at[1]),
    )
    for spot, target, copy in (
        (slice(channels, None), first, copies[0]),
        (slice(0, channels), second, copies[1]),
    ):
        value = value_ref[:, spot].astype(jnp.float32) * factor
        other = other_ref[:, spot].astype(jnp.float32) * factor
        target[:half, :] = jnp.where(mine == 0, value, other)
        target[half:, :] = jnp.where(mine == 0, other, value)
        copy.start()
    for copy in copies:
        copy.wait()


def digits(size):
    found = []
    factor = 2
    while size > 1:
        while size % factor == 0:
            found.append(factor)
            size //= factor
        factor += 1
    return found


def plan(n_outer, n_inner):
    steps = []
    stride = 1
    for size in (n_inner, n_outer):
        for radix in digits(size):
            steps.append((stride, radix))
            stride *= radix
    return steps


def linear_index():
    return lax.axis_index("outer") * lax.axis_size("inner") + lax.axis_index("inner")


def shifted(value, count, stride, radix, amount):
    perm = []
    for source in range(count):
        digit = (source // stride) % radix
        target = source + ((digit + amount) % radix - digit) * stride
        perm.append((source, target))
    return lax.ppermute(value, ("outer", "inner"), perm)


def turn(value, count, stride, radix):
    sent = value.astype(jnp.bfloat16)
    mine = (linear_index() // stride) % radix
    parts = jnp.stack([sent] + [shifted(sent, count, stride, radix, k) for k in range(1, radix)])
    total = jnp.zeros(value.shape, jnp.float32)
    for owner in range(radix):
        total = total + parts[(mine - owner) % radix].astype(jnp.float32)
    return total


def swap_stages(steps):
    masks = [stride for stride, radix in steps if radix == 2]
    even = len(masks) // 2 * 2
    return [masks[k : k + 2] for k in range(0, even, 2)], [[mask] for mask in masks[even:]]


def swap_sum(value, count, orders):
    sent = value.astype(jnp.bfloat16)

    def partner(pick):
        masks = []
        for stage in orders:
            mask = 0
            for k in pick:
                mask ^= stage[k]
            masks.append(mask)
        perm = [(source, source ^ masks[source % 2]) for source in range(count)]
        return lax.ppermute(sent, ("outer", "inner"), perm).astype(jnp.float32)

    if len(orders[0]) == 1:
        return sent.astype(jnp.float32) + partner((0,))
    near, far, both = partner((0,)), partner((1,)), partner((0, 1))
    return (sent.astype(jnp.float32) + near) + (far + both)


def pair_perm(count):
    return [(source, source ^ 1) for source in range(count)]


def exchange(keep, give):
    n_outer, n_inner = lax.axis_size("outer"), lax.axis_size("inner")
    count = n_outer * n_inner
    steps = plan(n_outer, n_inner)[1:]
    got = lax.ppermute(give, ("outer", "inner"), pair_perm(count))
    value = keep + got.astype(jnp.float32)
    quads, singles = swap_stages(steps)
    cut = len(quads) // 2
    for even, odd in zip(quads + singles, quads[cut:] + quads[:cut] + singles):
        value = swap_sum(value, count, (even, odd))
    for stride, radix in steps:
        if radix != 2:
            value = turn(value, count, stride, radix)
    value = value.astype(jnp.bfloat16)
    other = lax.ppermute(value, ("outer", "inner"), pair_perm(count))
    return value, other


VMEM = pl.BlockSpec(memory_space=pltpu.VMEM)
HBM = pl.BlockSpec(memory_space=pltpu.HBM)


def stay(value):
    return pltpu.with_memory_space_constraint(value, pltpu.HBM)


def shards(
    images,
    cotangent,
    conv_weight,
    conv_bias,
    norm_gain,
    norm_bias,
    expand_weight,
    expand_bias,
    reduce_weight,
    layer_scale,
    right_first,
    right_second,
):
    count = lax.axis_size("outer") * lax.axis_size("inner")
    scale = 1.0 / count
    extent, width = images.shape[1], images.shape[3]
    kernel = conv_weight.shape[0]
    hidden_units = expand_weight.shape[1]
    rank = right_first.shape[1]
    rows, half, total = extent * ROW, rank // 2, width + hidden_units
    slabs = width // LANES
    bf16, f32 = jnp.bfloat16, jnp.float32
    keep, give, normed, activated, grad, hid = pl.pallas_call(
        phase_one,
        out_shape=(
            jax.ShapeDtypeStruct((half, total), f32),
            jax.ShapeDtypeStruct((half, total), bf16),
            jax.ShapeDtypeStruct((rows, width), bf16),
            jax.ShapeDtypeStruct((rows, hidden_units), bf16),
            jax.ShapeDtypeStruct((rows, width), bf16),
            jax.ShapeDtypeStruct((rows, hidden_units), bf16),
        ),
        in_specs=[HBM] * 12,
        out_specs=(VMEM,) * 6,
        scratch_shapes=[
            pltpu.VMEM(images.shape[1:], bf16),
            pltpu.VMEM(images.shape[1:], bf16),
            pltpu.VMEM(conv_weight.shape, f32),
            pltpu.VMEM((width,), f32),
            pltpu.VMEM((width,), f32),
            pltpu.VMEM((width,), f32),
            pltpu.VMEM((width,), f32),
            pltpu.VMEM((hidden_units,), f32),
            pltpu.VMEM((slabs, extent + kernel - 1, 2 * ROW, LANES), f32),
            pltpu.VMEM((slabs, rows, LANES), f32),
            pltpu.VMEM(expand_weight.shape, bf16),
            pltpu.VMEM(reduce_weight.shape, bf16),
            pltpu.VMEM((rows, hidden_units), f32),
            pltpu.VMEM((rank, hidden_units), f32),
            pltpu.VMEM((rank, width), f32),
            pltpu.VMEM((half, total), f32),
            pltpu.VMEM((half, total), f32),
            pltpu.SemaphoreType.DMA((11,)),
            pltpu.SemaphoreType.DMA((hidden_units // BLOCK,)),
        ],
        compiler_params=pltpu.CompilerParams(vmem_limit_bytes=40 * 1024 * 1024),
        name="phase_one",
    )(
        stay(images),
        stay(cotangent),
        stay(conv_weight),
        stay(conv_bias),
        stay(norm_gain),
        stay(norm_bias),
        stay(expand_weight),
        stay(expand_bias),
        stay(reduce_weight),
        stay(layer_scale),
        stay(right_first.T),
        stay(right_second.T),
    )
    value, other = exchange(keep, give)
    keep, give = pl.pallas_call(
        phase_two,
        out_shape=(
            jax.ShapeDtypeStruct((half, total), f32),
            jax.ShapeDtypeStruct((half, total), bf16),
        ),
        in_specs=[VMEM] * 6,
        out_specs=(VMEM, VMEM),
        compiler_params=pltpu.CompilerParams(vmem_limit_bytes=40 * 1024 * 1024),
        name="phase_two",
    )(value, other, normed, activated, grad, hid)
    value, other = exchange(keep, give)
    second, first = pl.pallas_call(
        functools.partial(phase_three, 0.5 * scale),
        out_shape=(
            jax.ShapeDtypeStruct((rank, width), f32),
            jax.ShapeDtypeStruct((rank, hidden_units), f32),
        ),
        in_specs=[VMEM, VMEM],
        out_specs=(HBM, HBM),
        scratch_shapes=[
            pltpu.VMEM((rank, width), f32),
            pltpu.VMEM((rank, hidden_units), f32),
            pltpu.SemaphoreType.DMA((2,)),
        ],
        compiler_params=pltpu.CompilerParams(vmem_limit_bytes=8 * 1024 * 1024),
        name="phase_three",
    )(value, other)
    return (first.T, second.T)


def solution(mesh):
    in_specs = (
        P(("outer", "inner"), None, None, None),
        P(("outer", "inner"), None, None, None),
        P(),
        P(),
        P(),
        P(),
        P(),
        P(),
        P(),
        P(),
        P(),
        P(),
    )
    out_specs = (P(), P())
    return jax.shard_map(shards, mesh=mesh, in_specs=in_specs, out_specs=out_specs, check_vma=False)
```
